32 devices in a mesh: section: 8 (over y, x, core), replica: 4 (over z).
Axes of the slice: x: 2, y: 2, z: 4, core: 2. Of those that a mesh axis runs over, the one named last changes fastest.
Arguments:
- saved: bfloat16 [8, 2, 4, 4096, 128], P('section', None, 'replica'), may hold values from -6 to 6
- upstream: bfloat16 [8, 4, 4096, 128], P('section', 'replica'), may hold values from -0.59765625 to 0.59765625
- short_filters: float32 [8, 3, 256, 7], P('section'), may hold values from -2 to 2
- medium_filter: float32 [8, 256, 128], P('section'), may hold values from -0.5 to 0.5
- skip: float32 [8, 4096], P('section'), may hold values from -4 to 4
Outputs:
- short_grad: float32 [8, 3, 256, 7], P('section')
- medium_grad: float32 [8, 256, 128], P('section')
- skip_grad: float32 [8, 4096], P('section')
The draws below stay inside these ranges and needn't reach their ends.
All inputs are finite; a program needn't handle non-finite values.
Results may differ from the reference program's by a relative error of at most 0.0056.
Values may be sent and summed in bfloat16 or wider, within the bound.
No kernel may reach another device: no remote copies, remote signals or barrier semaphores. Data moves between devices by JAX's collectives and lax.ppermute only.
A program may use at most 192 MiB of HBM per device.

```python
import jax
import jax.numpy as jnp
from jax import lax

C = 4096
GROUP = 16
SHORT = 7
TAPS = 128
TOK = 128
TICKS = 2
GROUPS = 256
SECTIONS = 8
REPLICAS = 4


def block_levels(stream_key, shape, pieces, low, high):
    def one(position, blocks):
        draws = jax.random.uniform(jax.random.fold_in(jax.random.fold_in(stream_key, 6), position), (blocks,), jnp.float32, low / len(pieces), high / len(pieces))
        return jnp.repeat(jnp.exp(draws), shape[position] // blocks).reshape((-1,) + (1,) * (len(shape) - position - 1))

    factor_of = one(*pieces[0])
    for cut in pieces[1:]:
        factor_of = factor_of * one(*cut)
    return factor_of


def noise(rng, dims, spread, reach, shards=(), held_as=jnp.bfloat16):
    array = jax.random.normal(rng, dims, jnp.float32) * spread
    if len(shards) > 0:
        array = block_levels(rng, dims, shards, -0.22, 0.18) * array
    return jnp.clip(array, min=-reach, max=reach).astype(held_as)


def setup_inputs(seed: int = 0) -> dict:
    key_list = jax.random.split(jax.random.key(seed), 6)
    saved = noise(key_list[0], (SECTIONS, TICKS, REPLICAS, C, TOK), 1.0, 6.0, ((0, 8), (2, 4)))
    upstream = noise(key_list[1], (SECTIONS, REPLICAS, C, TOK), 0.1, 0.59765625, ((0, 8), (1, 4)))
    short_filters = noise(key_list[2], (SECTIONS, 3, GROUPS, SHORT), SHORT ** -0.5, 2.0, ((0, 8),), jnp.float32)
    medium_filter = noise(key_list[3], (SECTIONS, GROUPS, TAPS), TAPS ** -0.5, 0.5, ((0, 8),), jnp.float32)
    skip = noise(key_list[4], (SECTIONS, C), 1.0, 4.0, ((0, 8),), jnp.float32)
    return {"saved": saved, "upstream": upstream, "short_filters": short_filters, "medium_filter": medium_filter, "skip": skip}


PRECISE = lax.Precision.HIGHEST

def build_toeplitz(filter_low, length):
    tap_count = filter_low.shape[1]
    row_index = jnp.arange(length, dtype=jnp.int32)[:, None]
    col_index = jnp.arange(length, dtype=jnp.int32)[None, :]
    offsets = (col_index - row_index).astype(jnp.int32)
    inside = (offsets >= 0) & (offsets < tap_count)
    picked = jnp.take(filter_low, jnp.clip(offsets, 0, tap_count - 1).astype(jnp.int32), axis=1)
    return jnp.where(inside[None], picked, jnp.zeros((), filter_low.dtype))

def diagonal_sums(lag_products, tap_count):
    groups, length, _ = lag_products.shape
    flattened = lag_products.reshape(groups, length * length)
    flattened = jnp.pad(flattened, ((0, 0), (0, length)))
    skewed = flattened.reshape(groups, length, length + 1)[:, :, :tap_count]
    row_index = jnp.arange(length, dtype=jnp.int32)[:, None]
    lag_grid = jnp.arange(tap_count, dtype=jnp.int32)[None, :]
    within = row_index + lag_grid < length
    return lax.optimization_barrier(jnp.sum(jnp.where(within[None], skewed, jnp.zeros((), lag_products.dtype)), axis=1))

def short_forward(inputs, channel_filters):
    tap_count = channel_filters.shape[2]
    length = inputs.shape[1]
    padded = jnp.pad(inputs, ((0, 0), (tap_count - 1, 0)))
    running = jnp.zeros((channel_filters.shape[0],) + inputs.shape, jnp.float32)
    for lag_index in range(tap_count):
        start = tap_count - 1 - lag_index
        running = running + channel_filters[:, :, lag_index:lag_index + 1] * padded[None, :, start:start + length]
    return running

def short_transpose(grad_feats, channel_filters):
    tap_count = channel_filters.shape[2]
    length = grad_feats.shape[2]
    padded = jnp.pad(grad_feats, ((0, 0), (0, 0), (0, tap_count - 1)))
    running = jnp.zeros(grad_feats.shape[1:], jnp.float32)
    for lag_index in range(tap_count):
        running = running + lax.optimization_barrier(jnp.sum(channel_filters[:, :, lag_index:lag_index + 1] * padded[:, :, lag_index:lag_index + length], axis=0))
    return running

def short_filter_grad(grad_feats, inputs, tap_count):
    length = inputs.shape[1]
    padded = jnp.pad(inputs, ((0, 0), (tap_count - 1, 0)))
    columns = []
    for lag_index in range(tap_count):
        start = tap_count - 1 - lag_index
        columns.append(lax.optimization_barrier(jnp.sum(grad_feats * padded[None, :, start:start + length], axis=2)))
    return jnp.stack(columns, axis=2)

def contract(form, left, right):
    return jnp.einsum(form, left.astype(jnp.float32), right.astype(jnp.float32), precision=PRECISE)

def micro_backward(saved_rows, incoming, channel_filters, toeplitz, skip_row, need_grad):
    inputs = saved_rows.astype(jnp.float32)
    channels, length = inputs.shape
    groups = toeplitz.shape[0]
    features = short_forward(inputs, channel_filters)
    queries, key_feats, value_feats = (features[0], features[1], features[2])
    product = key_feats * value_feats
    product_low = lax.optimization_barrier(product.astype(jnp.bfloat16)).reshape(groups, channels // groups, length)
    conv_part = contract('gci,gio->gco', product_low, toeplitz).reshape(channels, length)
    mixed_out = conv_part + skip_row[:, None] * product
    cotangent = incoming.astype(jnp.float32)
    grad_query = cotangent * mixed_out
    grad_mixed = cotangent * queries
    grad_low = lax.optimization_barrier(grad_mixed.astype(jnp.bfloat16)).reshape(groups, channels // groups, length)
    back_part = contract('gco,gio->gci', grad_low, toeplitz).reshape(channels, length)
    grad_product = back_part + skip_row[:, None] * grad_mixed
    grad_feats = jnp.stack([grad_query, grad_product * value_feats, grad_product * key_feats])
    lag_products = contract('gci,gco->gio', product_low, grad_low)
    medium_term = diagonal_sums(lag_products, TAPS)
    short_term = short_filter_grad(grad_feats, inputs, channel_filters.shape[2])
    short_term = short_term.reshape(3, groups, channels // groups, -1).sum(axis=2)
    skip_term = lax.optimization_barrier(jnp.sum(grad_mixed * product, axis=1))
    grad_input = None
    if need_grad:
        grad_input = (cotangent + short_transpose(grad_feats, channel_filters)).astype(jnp.bfloat16)
    return (grad_input, short_term, medium_term, skip_term)

def reference(saved, upstream, short_filters, medium_filter, skip):
    tick_count = saved.shape[1]
    replicas = saved.shape[2]
    length = saved.shape[4]
    incoming = upstream
    totals = None
    for tick_index in range(tick_count):
        need_grad = tick_index + 1 < tick_count

        def per_section(section_items):
            saved_rows, section_incoming, section_short, section_medium, skip_row = section_items
            channel_filters = jnp.repeat(section_short, GROUP, axis=1)
            filter_low = lax.optimization_barrier(section_medium.astype(jnp.bfloat16))
            toeplitz = build_toeplitz(filter_low, length)

            def per_replica(replica_rows, replica_cot):
                return micro_backward(replica_rows, replica_cot, channel_filters, toeplitz, skip_row, need_grad)
            results = jax.vmap(per_replica)(saved_rows, section_incoming)
            summed = tuple((lax.optimization_barrier(jnp.sum(member, axis=0)) for member in results[1:]))
            return (results[0],) + summed
        section_out = lax.map(per_section, (saved[:, tick_index], incoming, short_filters, medium_filter, skip))
        tick_terms = section_out[1:]
        totals = tick_terms if totals is None else jax.tree.map(jnp.add, totals, tick_terms)
        if need_grad:
            passed = section_out[0]
            incoming = jnp.concatenate([passed[1:], jnp.zeros_like(passed[:1])], axis=0)
    inverse_count = 1.0 / replicas
    return (totals[0] * inverse_count, totals[1] * inverse_count, totals[2] * inverse_count)
```

```python
import functools

import jax
import jax.numpy as jnp
import numpy as np
from jax import lax
from jax.experimental import pallas as pl
from jax.experimental.pallas import tpu as pltpu
from jax.sharding import PartitionSpec as P

GROUP = 16
LANES = 128
SUB = 128

F32 = jnp.float32
BF16 = jnp.bfloat16
PRECISE = lax.Precision.HIGHEST


def shifted(array, axis, by):
    count = lax.axis_size(axis)
    pairs = [(i, i + by) for i in range(count) if 0 <= i + by < count]
    return lax.ppermute(array, axis, pairs)


def split(matrix):
    high = matrix.astype(jnp.bfloat16)
    low = (matrix - high.astype(np.float64)).astype(jnp.bfloat16)
    return high, low


@functools.lru_cache(None)
def tables(length, taps):
    points = 2 * length
    pos = np.arange(length)[:, None]
    freq = np.arange(length)[None, :]
    angle = 2.0 * np.pi * ((pos * freq) % points) / points
    real, imag = np.cos(angle), -np.sin(angle)
    imag[:, 0] = 1.0 - 2.0 * (np.arange(length) % 2)
    forward = np.concatenate([real, imag], axis=1)
    weight = np.full((2 * length, 1), 2.0 / points)
    weight[0] = weight[length] = 1.0 / points
    inverse = weight * forward.T
    shift = np.concatenate([np.eye(length, k=lag) for lag in range(1, taps)], axis=1)
    unshift = np.concatenate([np.eye(length, k=-lag) for lag in range(taps)], axis=0)
    return (
        np.concatenate(split(forward), axis=0),
        np.concatenate(split(inverse), axis=0),
        inverse.astype(np.float32),
        shift.astype(jnp.bfloat16),
        unshift.astype(jnp.bfloat16),
    )


def nt(left, right, precision=None):
    return lax.dot_general(
        left, right, (((1,), (1,)), ((), ())), precision=precision, preferred_element_type=F32
    )


def mm(left, right, precision=None):
    return jnp.dot(left, right, precision=precision, preferred_element_type=F32)


def row(ref, *index):
    return jnp.broadcast_to(ref[index], (GROUP, LANES))


def tick_kernel(last, taps, *refs):
    if last:
        (x_ref, cot_ref, f_ref, med_ref, skip_ref, fwd_ref, inv_ref, shift_ref, finv_ref,
         acc_in, skip_in, msg_ref, fsp, coef, xs, feat, hat, res, red, acc, skips) = refs
    else:
        (x_ref, cot_ref, f_ref, med_ref, skip_ref, fwd_ref, inv_ref, shift_ref, unshift_ref,
         gin_ref, acc, skips, fsp, coef, xs, feat, hat, res, red) = refs
    channels = x_ref.shape[-2]
    groups = channels // GROUP
    ng = SUB // GROUP
    lane = lax.broadcasted_iota(jnp.int32, (1, LANES), 1)
    first = lane == 0

    h = med_ref[0].astype(BF16)
    hh = mm(jnp.concatenate([h, h], axis=1), fwd_ref[...])
    hr, hi = hh[:, :LANES], hh[:, LANES:]
    coef[0] = hr
    coef[1] = jnp.where(first, 0.0, hi)
    coef[2] = jnp.where(first, hi, hr)

    def block(index, _):
        base = pl.multiple_of(index * SUB, SUB)
        gbase = pl.multiple_of(index * ng, ng)
        rows = pl.ds(base, SUB)
        own = lax.rem(lax.broadcasted_iota(jnp.int32, (GROUP, LANES), 1), GROUP) == (
            lax.broadcasted_iota(jnp.int32, (GROUP, LANES), 0)
        )
        x = x_ref[0, 0, 0, rows, :]
        xs[:, LANES:] = mm(x, shift_ref[...])
        xs[:, :LANES] = x.astype(F32)
        for m in range(3):
            taps_m = f_ref[0, m, pl.ds(gbase, ng), :]
            for j in range(taps):
                fsp[m * taps + j] = jnp.broadcast_to(taps_m[:, j : j + 1], (ng, LANES))
        local = [coef[i, pl.ds(gbase, ng), :] for i in range(3)]
        for i in range(3):
            red[i, :ng, :] = local[i]
        skip_cols = jnp.broadcast_to(skip_ref[pl.ds(index, 1), :], (SUB, LANES)).T

        lows, grads = [], []
        for k in range(ng):
            r = slice(GROUP * k, GROUP * (k + 1))
            f = [None] * 3
            for m in range(3):
                total = None
                for j in range(taps):
                    term = row(fsp, m * taps + j, slice(k, k + 1)) * xs[r, LANES * j : LANES * (j + 1)]
                    total = term if total is None else total + term
                f[m] = total
            product = f[1] * f[2]
            cot = cot_ref[pl.ds(base + GROUP * k, GROUP), :].astype(F32)
            gm = cot * f[0]
            feat[0, r] = f[1]
            feat[1, r] = f[2]
            feat[2, r] = product
            feat[3, r] = gm
            lows.append(product.astype(BF16))
            grads.append(gm.astype(BF16))
        both = jnp.concatenate(lows + grads, axis=0)
        hat[...] = mm(jnp.concatenate([both, both], axis=1), fwd_ref[...])

        conv_in, back_in = [], []
        for k in range(ng):
            r = slice(GROUP * k, GROUP * (k + 1))
            rg = slice(SUB + GROUP * k, SUB + GROUP * (k + 1))
            ca, cb, cc = (row(red, i, slice(k, k + 1)) for i in range(3))
            pr, pi = hat[r, :LANES], hat[r, LANES:]
            gr, gi = hat[rg, :LANES], hat[rg, LANES:]
            conv_in.append(
                jnp.concatenate([pr * ca - pi * cb, pr * cb + pi * cc], axis=1).astype(BF16)
            )
            back_in.append(
                jnp.concatenate([gr * ca + gi * cb, gi * cc - gr * cb], axis=1).astype(BF16)
            )
            for i, value in enumerate((pr * gr, pi * gi, pr * gi - pi * gr)):
                red[3 + i, 8 * k : 8 * k + 8, :] = value[:8] + value[8:]
        spec = jnp.concatenate(conv_in + back_in, axis=0)
        res[...] = mm(jnp.concatenate([spec, spec], axis=1), inv_ref[...])

        sums = []
        for k in range(ng):
            r = slice(GROUP * k, GROUP * (k + 1))
            rg = slice(SUB + GROUP * k, SUB + GROUP * (k + 1))
            cot = cot_ref[pl.ds(base + GROUP * k, GROUP), :].astype(F32)
            kf, vf, product, gm = (feat[i, r] for i in range(4))
            sk = skip_cols[r]
            gq = cot * (res[r] + sk * product)
            gp = res[rg] + sk * gm
            gf = [gq, gp * vf, gp * kf]
            sums.append((gm * product).astype(BF16))
            gfb = jnp.concatenate([g.astype(BF16) for g in gf], axis=0)
            xsb = jnp.concatenate(
                [xs[r, LANES * j : LANES * (j + 1)].astype(BF16) for j in range(taps)]
                + [jnp.zeros((GROUP, LANES), BF16)] * (LANES // GROUP - taps),
                axis=0,
            )
            corr = nt(gfb, xsb)
            for m in range(3):
                kept = jnp.where(own, corr[GROUP * m : GROUP * (m + 1)], 0.0)
                red[6 + m, 8 * k : 8 * k + 8, :] = kept[:8] + kept[8:]
            if not last:
                parts = []
                for j in range(taps):
                    total = None
                    for m in range(3):
                        term = row(fsp, m * taps + j, slice(k, k + 1)) * gf[m]
                        total = term if total is None else total + term
                    parts.append(total.astype(BF16))
                hats = jnp.concatenate(parts, axis=1)
                gin = cot + mm(hats, unshift_ref[...])
                gin_ref[pl.ds(base + GROUP * k, GROUP), :] = gin.astype(BF16)
        for i in range(6):
            total = red[3 + i, pl.ds(0, ng, stride=8), :]
            for s in range(1, 8):
                total = total + red[3 + i, pl.ds(s, ng, stride=8), :]
            acc[i, pl.ds(gbase, ng), :] = total
        ones = jnp.ones((8, LANES), BF16)
        skips[pl.ds(index, 1), :] = nt(ones, jnp.concatenate(sums, axis=0))[:1]
        return 0

    lax.fori_loop(0, channels // SUB, block, 0)

    if last:
        total = [acc[i] + acc_in[i] for i in range(6)]
        real = total[0] + jnp.where(first, 0.0, total[1])
        imag = jnp.where(first, total[1], total[2])
        msg_ref[:groups] = mm(jnp.concatenate([real, imag], axis=1), finv_ref[...], PRECISE)
        at = groups
        count = channels // LANES
        msg_ref[at : at + count] = skips[...] + skip_in[...]
        at += count
        pick = (
            lax.broadcasted_iota(jnp.int32, (8, LANES), 1) // GROUP
            == lax.broadcasted_iota(jnp.int32, (8, LANES), 0)
        ).astype(F32)
        for m in range(3):
            for q in range(groups // LANES):
                part = total[3 + m][LANES * q : LANES * (q + 1)]
                msg_ref[at : at + 8] = nt(pick, part, PRECISE)
                at += 8


def run_tick(saved, cot, filters, medium, skip_rows, tick, prior):
    last = prior is not None
    channels, length = saved.shape[-2:]
    groups = filters.shape[2]
    taps = filters.shape[3]
    forward, inverse, inverse_full, shift, unshift = tables(length, taps)
    ng = SUB // GROUP
    full = lambda a: pl.BlockSpec(a.shape, lambda i: (0,) * a.ndim)
    x_spec = pl.BlockSpec((1, 1, 1, channels, length), lambda i: (0, tick, 0, 0, 0))
    ins = [saved, cot, filters, medium, skip_rows, forward, inverse, shift]
    ins += [inverse_full, *prior] if last else [unshift]
    acc_shape = (6, groups, LANES)
    skip_shape = (channels // LANES, LANES)
    scratch = [
        pltpu.VMEM((3 * taps, ng, LANES), F32),
        pltpu.VMEM((3, groups, LANES), F32),
        pltpu.VMEM((SUB, taps * LANES), F32),
        pltpu.VMEM((4, SUB, LANES), F32),
        pltpu.VMEM((2 * SUB, 2 * LANES), F32),
        pltpu.VMEM((2 * SUB, LANES), F32),
        pltpu.VMEM((9, 8 * ng, LANES), F32),
    ]
    if last:
        outs = [jax.ShapeDtypeStruct((groups + channels // LANES + 24 * (groups // LANES), LANES), F32)]
        scratch += [pltpu.VMEM(acc_shape, F32), pltpu.VMEM(skip_shape, F32)]
    else:
        outs = [
            jax.ShapeDtypeStruct((channels, length), BF16),
            jax.ShapeDtypeStruct(acc_shape, F32),
            jax.ShapeDtypeStruct(skip_shape, F32),
        ]
    return pl.pallas_call(
        functools.partial(tick_kernel, last, taps),
        out_shape=outs,
        grid=(1,),
        in_specs=[x_spec] + [full(a) for a in ins[1:]],
        out_specs=[full(a) for a in outs],
        scratch_shapes=scratch,
        compiler_params=pltpu.CompilerParams(vmem_limit_bytes=48 << 20),
        name="last_tick" if last else "first_tick",
    )(*ins)


def finish_kernel(count, taps, *refs):
    ins, (short_ref, medium_ref, skip_ref) = refs[:count], refs[count:]
    total = ins[0][...]
    for ref in ins[1:]:
        total = total + ref[...]
    total = total * (1.0 / count)
    groups = medium_ref.shape[1]
    channels = skip_ref.shape[1]
    medium_ref[0] = total[:groups]
    at = groups
    for i in range(channels // LANES):
        skip_ref[:, LANES * i : LANES * (i + 1)] = total[at : at + 1]
        at += 1
    for m in range(3):
        for q in range(groups // LANES):
            short_ref[0, m, LANES * q : LANES * (q + 1), :] = total[at : at + 8].T[:, :taps]
            at += 8


def finish(parts, groups, channels, taps):
    return pl.pallas_call(
        functools.partial(finish_kernel, len(parts), taps),
        out_shape=(
            jax.ShapeDtypeStruct((1, 3, groups, taps), F32),
            jax.ShapeDtypeStruct((1, groups, LANES), F32),
            jax.ShapeDtypeStruct((1, channels), F32),
        ),
        name="finish",
    )(*parts)


def body(saved, upstream, short_filters, medium_filter, skip):
    channels, length = saved.shape[-2:]
    ticks = saved.shape[1]
    groups, taps = short_filters.shape[2:]
    replicas = lax.axis_size("replica")
    skip_rows = skip.reshape(channels // LANES, LANES)
    incoming = upstream[0, 0]
    gin, acc, skips = run_tick(saved, incoming, short_filters, medium_filter, skip_rows, 0, None)
    incoming = shifted(gin, "section", -1)
    (message,) = run_tick(
        saved, incoming, short_filters, medium_filter, skip_rows, 1, (acc, skips)
    )
    parts = [message] + [
        lax.ppermute(message, "replica", [(i, (i + by) % replicas) for i in range(replicas)])
        for by in range(1, replicas)
    ]
    return finish(parts, groups, channels, taps)


def solution(mesh):
    placed = (
        P("section", None, "replica", None, None),
        P("section", "replica", None, None),
        P("section", None, None, None),
        P("section", None, None),
        P("section", None),
    )
    return jax.shard_map(
        body,
        mesh=mesh,
        in_specs=placed,
        out_specs=(P("section", None, None, None), P("section", None, None), P("section", None)),
        check_vma=False,
    )
```

```python
import functools

import jax
import jax.numpy as jnp
import numpy as np
from jax import lax
from jax.experimental import pallas as pl
from jax.experimental.pallas import tpu as pltpu
from jax.sharding import PartitionSpec as P

GROUP = 16
LANES = 128
SUB = 128

F32 = jnp.float32
BF16 = jnp.bfloat16
PRECISE = lax.Precision.HIGHEST


def shifted(array, axis, by):
    count = lax.axis_size(axis)
    pairs = [(i, i + by) for i in range(count) if 0 <= i + by < count]
    return lax.ppermute(array, axis, pairs)


def split(matrix):
    high = matrix.astype(jnp.bfloat16)
    low = (matrix - high.astype(np.float64)).astype(jnp.bfloat16)
    return high, low


@functools.lru_cache(None)
def tables(length, taps):
    points = 2 * length
    pos = np.arange(length)[:, None]
    freq = np.arange(length)[None, :]
    angle = 2.0 * np.pi * ((pos * freq) % points) / points
    real, imag = np.cos(angle), -np.sin(angle)
    imag[:, 0] = 1.0 - 2.0 * (np.arange(length) % 2)
    forward = np.concatenate([real, imag], axis=1)
    weight = np.full((2 * length, 1), 2.0 / points)
    weight[0] = weight[length] = 1.0 / points
    inverse = weight * forward.T
    shift = np.concatenate([np.eye(length, k=lag) for lag in range(1, taps)], axis=1)
    unshift = np.concatenate([np.eye(length, k=-lag) for lag in range(taps)], axis=0)
    return (
        np.concatenate(split(forward), axis=0),
        np.concatenate(split(inverse), axis=0),
        inverse.astype(np.float32),
        shift.astype(jnp.bfloat16),
        unshift.astype(jnp.bfloat16),
    )


def nt(left, right, precision=None):
    return lax.dot_general(
        left, right, (((1,), (1,)), ((), ())), precision=precision, preferred_element_type=F32
    )


def mm(left, right, precision=None):
    return jnp.dot(left, right, precision=precision, preferred_element_type=F32)


def row(ref, *index):
    return jnp.broadcast_to(ref[index], (GROUP, LANES))


def own_channel():
    lane = lax.broadcasted_iota(jnp.int32, (GROUP, LANES), 1)
    return lax.rem(lane, GROUP) == lax.broadcasted_iota(jnp.int32, (GROUP, LANES), 0)


class Tick:
    def __init__(self, last, taps, ins, outs, scratch):
        self.last, self.taps, self.ng = last, taps, SUB // GROUP
        (self.x, self.cot, self.f, self.med, self.skip, self.fwd, self.inv, self.shift) = ins[:8]
        if last:
            (self.finv, self.acc_in, self.skip_in) = ins[8:]
            (self.msg,) = outs
            self.acc, self.skips = scratch[-2:]
        else:
            (self.unshift,) = ins[8:]
            self.gin, self.acc, self.skips = outs
        self.columns, self.coef = scratch[:2]
        self.slots = (scratch[2:9], scratch[9:16])
        self.spec, self.res, self.red, self.sums, self.hats, self.turn = scratch[16:22]

    def rows(self, block):
        return pl.multiple_of(block * SUB, SUB)

    def groups(self, block):
        return pl.ds(pl.multiple_of(block * self.ng, self.ng), self.ng)

    def setup(self):
        first = lax.broadcasted_iota(jnp.int32, (1, LANES), 1) == 0
        h = self.med[0].astype(BF16)
        hh = mm(jnp.concatenate([h, h], axis=1), self.fwd[...])
        hr, hi = hh[:, :LANES], hh[:, LANES:]
        self.coef[0] = hr
        self.coef[1] = jnp.where(first, 0.0, hi)
        self.coef[2] = jnp.where(first, hi, hr)
        self.turn[...] = jnp.zeros_like(self.turn)
        for q in range(h.shape[0] // LANES):
            cols = slice(LANES * q, LANES * (q + 1))
            for m in range(3):
                for j in range(self.taps):
                    t = m * self.taps + j
                    self.turn[t : t + 1, :] = self.f[m, j, :, cols]
            self.columns[cols, :] = self.turn[...].T

    def start(self, block, slot):
        taps_at, coef_at, skip_at, xs, _, _, _ = self.slots[slot]
        x = self.x[0, 0, 0, pl.ds(self.rows(block), SUB), :]
        xs[:, LANES:] = mm(x, self.shift[...])
        xs[:, :LANES] = x.astype(F32)
        mine = self.columns[self.groups(block), :]
        for t in range(3 * self.taps):
            taps_at[t] = jnp.broadcast_to(mine[:, t : t + 1], (self.ng, LANES))
        for i in range(3):
            coef_at[i] = self.coef[i, self.groups(block), :]
        skip_at[...] = jnp.broadcast_to(self.skip[pl.ds(block, 1), :], (SUB, LANES)).T

    def features(self, block, slot):
        taps_at, _, _, xs, feat, lows, _ = self.slots[slot]
        for k in range(self.ng):
            r = slice(GROUP * k, GROUP * (k + 1))
            rg = slice(SUB + GROUP * k, SUB + GROUP * (k + 1))
            f = []
            for m in range(3):
                total = None
                for j in range(self.taps):
                    tap = row(taps_at, m * self.taps + j, slice(k, k + 1))
                    term = tap * xs[r, LANES * j : LANES * (j + 1)]
                    total = term if total is None else total + term
                f.append(total)
            product = f[1] * f[2]
            gm = self.cot[pl.ds(self.rows(block) + GROUP * k, GROUP), :].astype(F32) * f[0]
            feat[0, r] = f[1]
            feat[1, r] = f[2]
            feat[2, r] = product
            feat[3, r] = gm
            lows[r] = product.astype(BF16)
            lows[rg] = gm.astype(BF16)

    def spectra(self, slot):
        lows, hat = self.slots[slot][5:]
        low = lows[...]
        hat[...] = mm(jnp.concatenate([low, low], axis=1), self.fwd[...])

    def filter(self, slot):
        _, coef_at, _, _, _, _, hat = self.slots[slot]
        spec, red = self.spec, self.red
        for k in range(self.ng):
            r = slice(GROUP * k, GROUP * (k + 1))
            rg = slice(SUB + GROUP * k, SUB + GROUP * (k + 1))
            ca, cb, cc = (row(coef_at, i, slice(k, k + 1)) for i in range(3))
            pr, pi = hat[r, :LANES], hat[r, LANES:]
            gr, gi = hat[rg, :LANES], hat[rg, LANES:]
            spec[r, :LANES] = (pr * ca - pi * cb).astype(BF16)
            spec[r, LANES:] = (pr * cb + pi * cc).astype(BF16)
            spec[rg, :LANES] = (gr * ca + gi * cb).astype(BF16)
            spec[rg, LANES:] = (gi * cc - gr * cb).astype(BF16)
            for i, value in enumerate((pr * gr, pi * gi, pr * gi - pi * gr)):
                red[i, 8 * k : 8 * k + 8, :] = value[:8] + value[8:]

    def invert(self):
        both = self.spec[...]
        self.res[...] = mm(jnp.concatenate([both, both], axis=1), self.inv[...])

    def gradients(self, block, slot):
        taps_at, _, skip_at, xs, feat, _, _ = self.slots[slot]
        own = own_channel()
        for k in range(self.ng):
            r = slice(GROUP * k, GROUP * (k + 1))
            rg = slice(SUB + GROUP * k, SUB + GROUP * (k + 1))
            cot = self.cot[pl.ds(self.rows(block) + GROUP * k, GROUP), :].astype(F32)
            kf, vf, product, gm = (feat[i, r] for i in range(4))
            sk = skip_at[r]
            gq = cot * (self.res[r] + sk * product)
            gp = self.res[rg] + sk * gm
            gf = [gq, gp * vf, gp * kf]
            self.sums[r] = (gm * product).astype(BF16)
            gfb = jnp.concatenate([g.astype(BF16) for g in gf], axis=0)
            xsb = jnp.concatenate(
                [xs[r, LANES * j : LANES * (j + 1)].astype(BF16) for j in range(self.taps)]
                + [jnp.zeros((GROUP, LANES), BF16)] * (LANES // GROUP - self.taps),
                axis=0,
            )
            corr = nt(gfb, xsb)
            if not self.last:
                for j in range(self.taps):
                    total = None
                    for m in range(3):
                        tap = row(taps_at, m * self.taps + j, slice(k, k + 1))
                        total = tap * gf[m] if total is None else total + tap * gf[m]
                    self.hats[r, LANES * j : LANES * (j + 1)] = total.astype(BF16)
            for m in range(3):
                kept = jnp.where(own, corr[GROUP * m : GROUP * (m + 1)], 0.0)
                self.red[3 + m, 8 * k : 8 * k + 8, :] = kept[:8] + kept[8:]

    def reduce(self, block, terms):
        for i in terms:
            total = self.red[i, pl.ds(0, self.ng, stride=8), :]
            for s in range(1, 8):
                total = total + self.red[i, pl.ds(s, self.ng, stride=8), :]
            self.acc[i, self.groups(block), :] = total

    def finish(self, block):
        if not self.last:
            rows = pl.ds(self.rows(block), SUB)
            gin = mm(self.hats[...], self.unshift[...]) + self.cot[rows, :].astype(F32)
            self.gin[rows, :] = gin.astype(BF16)
        self.skips[pl.ds(block, 1), :] = nt(jnp.ones((8, LANES), BF16), self.sums[...])[:1]
        self.reduce(block, range(3, 6))

    def step(self, block, blocks, slot):
        after = jnp.minimum(block + 1, blocks - 1)
        self.start(after, 1 - slot)
        self.filter(slot)
        self.invert()
        self.finish(jnp.maximum(block - 1, 0))
        self.features(after, 1 - slot)
        self.reduce(block, range(3))
        self.spectra(1 - slot)
        self.gradients(block, slot)

    def message(self):
        first = lax.broadcasted_iota(jnp.int32, (1, LANES), 1) == 0
        total = [self.acc[i] + self.acc_in[i] for i in range(6)]
        real = total[0] + jnp.where(first, 0.0, total[1])
        imag = jnp.where(first, total[1], total[2])
        at = real.shape[0]
        both = jnp.concatenate([real, imag], axis=1)
        self.msg[:at] = mm(both, self.finv[...], PRECISE)
        count = self.skips.shape[0]
        self.msg[at : at + count] = self.skips[...] + self.skip_in[...]
        at += count
        pick = (
            lax.broadcasted_iota(jnp.int32, (8, LANES), 1) // GROUP
            == lax.broadcasted_iota(jnp.int32, (8, LANES), 0)
        ).astype(F32)
        for m in range(3):
            for q in range(real.shape[0] // LANES):
                part = total[3 + m][LANES * q : LANES * (q + 1)]
                self.msg[at : at + 8] = nt(pick, part, PRECISE)
                at += 8


def tick_kernel(last, taps, counts, *refs):
    ins, outs, scratch = refs[: counts[0]], refs[counts[0] : sum(counts)], refs[sum(counts) :]
    tick = Tick(last, taps, ins, outs, scratch)
    blocks = tick.x.shape[-2] // SUB
    tick.setup()
    tick.start(0, 0)
    tick.features(0, 0)
    tick.spectra(0)

    def pair(index, _):
        tick.step(2 * index, blocks, 0)
        tick.step(2 * index + 1, blocks, 1)
        return 0

    lax.fori_loop(0, blocks // 2, pair, 0)
    tick.finish(blocks - 1)
    if last:
        tick.message()


def in_hbm(array):
    return pltpu.with_memory_space_constraint(array, pltpu.HBM)


def run_tick(saved, cot, filters, medium, skip_rows, tick, prior):
    last = prior is not None
    channels, length = saved.shape[-2:]
    taps = filters.shape[1]
    groups = filters.shape[3]
    forward, inverse, inverse_full, shift, unshift = tables(length, taps)
    ng = SUB // GROUP
    full = lambda a: pl.BlockSpec(a.shape, lambda i: (0,) * a.ndim)
    x_spec = pl.BlockSpec((1, 1, 1, channels, length), lambda i: (0, tick, 0, 0, 0))
    ins = [saved, cot, filters, medium, skip_rows, forward, inverse, shift]
    ins += [inverse_full] if last else [unshift]
    ins = [in_hbm(jnp.asarray(a)) for a in ins]
    ins += [*prior] if last else []
    acc_shape = (6, groups, LANES)
    skip_shape = (channels // LANES, LANES)
    slot = [
        pltpu.VMEM((3 * taps, ng, LANES), F32),
        pltpu.VMEM((3, ng, LANES), F32),
        pltpu.VMEM((SUB, LANES), F32),
        pltpu.VMEM((SUB, taps * LANES), F32),
        pltpu.VMEM((4, SUB, LANES), F32),
        pltpu.VMEM((2 * SUB, LANES), BF16),
        pltpu.VMEM((2 * SUB, 2 * LANES), F32),
    ]
    scratch = [pltpu.VMEM((groups, LANES), F32), pltpu.VMEM((3, groups, LANES), F32)]
    scratch += slot + slot
    scratch += [
        pltpu.VMEM((2 * SUB, 2 * LANES), BF16),
        pltpu.VMEM((2 * SUB, LANES), F32),
        pltpu.VMEM((6, 8 * ng, LANES), F32),
        pltpu.VMEM((SUB, LANES), BF16),
        pltpu.VMEM((SUB, taps * LANES), BF16),
        pltpu.VMEM((LANES, LANES), F32),
    ]
    if last:
        outs = [jax.ShapeDtypeStruct((groups + channels // LANES + 24 * (groups // LANES), LANES), F32)]
        scratch += [pltpu.VMEM(acc_shape, F32), pltpu.VMEM(skip_shape, F32)]
    else:
        outs = [
            jax.ShapeDtypeStruct((channels, length), BF16),
            jax.ShapeDtypeStruct(acc_shape, F32),
            jax.ShapeDtypeStruct(skip_shape, F32),
        ]
    return pl.pallas_call(
        functools.partial(tick_kernel, last, taps, (len(ins), len(outs))),
        out_shape=outs,
        grid=(1,),
        in_specs=[x_spec] + [full(a) for a in ins[1:]],
        out_specs=[full(a) for a in outs],
        scratch_shapes=scratch,
        compiler_params=pltpu.CompilerParams(vmem_limit_bytes=48 << 20),
        name="last_tick" if last else "first_tick",
    )(*ins)


def finish_kernel(count, taps, *refs):
    ins, (short_ref, medium_ref, skip_ref) = refs[:count], refs[count:]
    total = ins[0][...]
    for ref in ins[1:]:
        total = total + ref[...]
    total = total * (1.0 / count)
    groups = medium_ref.shape[0]
    medium_ref[...] = total[:groups]
    at = groups + skip_ref.shape[0]
    skip_ref[...] = total[groups:at]
    for m in range(3):
        for q in range(groups // LANES):
            for j in range(taps):
                short_ref[m, j, :, LANES * q : LANES * (q + 1)] = total[at + j : at + j + 1]
            at += 8


def finish(parts, groups, channels, taps):
    vmem = pl.BlockSpec(memory_space=pltpu.VMEM)
    return pl.pallas_call(
        functools.partial(finish_kernel, len(parts), taps),
        out_shape=(
            jax.ShapeDtypeStruct((3, taps, 1, groups), F32),
            jax.ShapeDtypeStruct((groups, LANES), F32),
            jax.ShapeDtypeStruct((channels // LANES, LANES), F32),
        ),
        in_specs=[vmem] * len(parts),
        out_specs=[vmem] * 3,
        name="finish",
    )(*parts)


def body(saved, upstream, short_filters, medium_filter, skip):
    channels, length = saved.shape[-2:]
    groups, taps = short_filters.shape[2:]
    replicas = lax.axis_size("replica")
    skip_rows = skip.reshape(channels // LANES, LANES)
    filters = jnp.transpose(short_filters, (1, 3, 0, 2))
    incoming = upstream[0, 0]
    gin, acc, skips = run_tick(saved, incoming, filters, medium_filter, skip_rows, 0, None)
    incoming = shifted(gin, "section", -1)
    (message,) = run_tick(saved, incoming, filters, medium_filter, skip_rows, 1, (acc, skips))
    parts = [message] + [
        lax.ppermute(message, "replica", [(i, (i + by) % replicas) for i in range(replicas)])
        for by in range(1, replicas)
    ]
    short, medium, skip_grad = finish(parts, groups, channels, taps)
    return (
        jnp.transpose(short, (2, 0, 3, 1)),
        medium[None],
        skip_grad.reshape(1, channels),
    )


def solution(mesh):
    placed = (
        P("section", None, "replica", None, None),
        P("section", "replica", None, None),
        P("section", None, None, None),
        P("section", None, None),
        P("section", None),
    )
    return jax.shard_map(
        body,
        mesh=mesh,
        in_specs=placed,
        out_specs=(P("section", None, None, None), P("section", None, None), P("section", None)),
        check_vma=False,
    )
```

```python
import functools

import jax
import jax.numpy as jnp
import numpy as np
from jax import lax
from jax.experimental import pallas as pl
from jax.experimental.pallas import tpu as pltpu
from jax.sharding import PartitionSpec as P

GROUP = 16
LANES = 128
SUB = 128

F32 = jnp.float32
BF16 = jnp.bfloat16
PRECISE = lax.Precision.HIGHEST


def shifted(array, axis, by):
    count = lax.axis_size(axis)
    pairs = [(i, i + by) for i in range(count) if 0 <= i + by < count]
    return lax.ppermute(array, axis, pairs)


def split(matrix):
    high = matrix.astype(jnp.bfloat16)
    low = (matrix - high.astype(np.float64)).astype(jnp.bfloat16)
    return high, low


@functools.lru_cache(None)
def tables(length, taps):
    points = 2 * length
    pos = np.arange(length)[:, None]
    freq = np.arange(length)[None, :]
    angle = 2.0 * np.pi * ((pos * freq) % points) / points
    real, imag = np.cos(angle), -np.sin(angle)
    imag[:, 0] = 1.0 - 2.0 * (np.arange(length) % 2)
    forward = np.concatenate([real, imag], axis=1)
    weight = np.full((2 * length, 1), 2.0 / points)
    weight[0] = weight[length] = 1.0 / points
    inverse = weight * forward.T
    shift = np.concatenate([np.eye(length, k=lag) for lag in range(1, taps)], axis=1)
    unshift = np.concatenate([np.eye(length, k=-lag) for lag in range(taps)], axis=0)
    return (
        np.concatenate(split(forward), axis=0),
        np.concatenate(split(inverse), axis=0),
        inverse.astype(np.float32),
        shift.astype(jnp.bfloat16),
        unshift.astype(jnp.bfloat16),
    )


def nt(left, right, precision=None):
    return lax.dot_general(
        left, right, (((1,), (1,)), ((), ())), precision=precision, preferred_element_type=F32
    )


def mm(left, right, precision=None):
    return jnp.dot(left, right, precision=precision, preferred_element_type=F32)


def row(ref, *index):
    return jnp.broadcast_to(ref[index], (GROUP, LANES))


def own_channel():
    lane = lax.broadcasted_iota(jnp.int32, (GROUP, LANES), 1)
    return lax.rem(lane, GROUP) == lax.broadcasted_iota(jnp.int32, (GROUP, LANES), 0)


class Tick:
    def __init__(self, last, taps, ins, outs, scratch):
        self.last, self.taps, self.ng = last, taps, SUB // GROUP
        (self.x, self.cot, self.f, self.med, self.skip, self.fwd, self.inv, self.shift) = ins[:8]
        if last:
            self.finv, self.acc_in, self.skip_in, *self.earlier = ins[8:]
            (self.msg,) = outs
            self.acc, self.skips = scratch[-2:]
        else:
            (self.unshift,) = ins[8:]
            self.gin, self.acc, self.skips = outs
        self.columns, self.coef = scratch[:2]
        self.slots = (scratch[2:9], scratch[9:16])
        self.spec, self.res, self.red, self.sums, self.hats, self.turn = scratch[16:22]

    def rows(self, block):
        return pl.multiple_of(block * SUB, SUB)

    def groups(self, block):
        return pl.ds(pl.multiple_of(block * self.ng, self.ng), self.ng)

    def setup(self):
        first = lax.broadcasted_iota(jnp.int32, (1, LANES), 1) == 0
        h = self.med[0].astype(BF16)
        hh = mm(jnp.concatenate([h, h], axis=1), self.fwd[...])
        hr, hi = hh[:, :LANES], hh[:, LANES:]
        self.coef[0] = hr
        self.coef[1] = jnp.where(first, 0.0, hi)
        self.coef[2] = jnp.where(first, hi, hr)
        self.turn[...] = jnp.zeros_like(self.turn)
        for q in range(h.shape[0] // LANES):
            cols = slice(LANES * q, LANES * (q + 1))
            for m in range(3):
                for j in range(self.taps):
                    t = m * self.taps + j
                    self.turn[t : t + 1, :] = self.f[m, j, :, cols]
            self.columns[cols, :] = self.turn[...].T

    def start(self, block, slot):
        taps_at, coef_at, skip_at, xs, _, _, _ = self.slots[slot]
        x = self.x[0, 0, 0, pl.ds(self.rows(block), SUB), :]
        xs[:, LANES:] = mm(x, self.shift[...])
        xs[:, :LANES] = x.astype(F32)
        mine = self.columns[self.groups(block), :]
        for t in range(3 * self.taps):
            taps_at[t] = jnp.broadcast_to(mine[:, t : t + 1], (self.ng, LANES))
        for i in range(3):
            coef_at[i] = self.coef[i, self.groups(block), :]
        skip_at[...] = jnp.broadcast_to(self.skip[pl.ds(block, 1), :], (SUB, LANES)).T

    def features(self, block, slot):
        taps_at, _, _, xs, feat, lows, _ = self.slots[slot]
        for k in range(self.ng):
            r = slice(GROUP * k, GROUP * (k + 1))
            rg = slice(SUB + GROUP * k, SUB + GROUP * (k + 1))
            f = []
            for m in range(3):
                total = None
                for j in range(self.taps):
                    tap = row(taps_at, m * self.taps + j, slice(k, k + 1))
                    term = tap * xs[r, LANES * j : LANES * (j + 1)]
                    total = term if total is None else total + term
                f.append(total)
            product = f[1] * f[2]
            gm = self.cot[pl.ds(self.rows(block) + GROUP * k, GROUP), :].astype(F32) * f[0]
            feat[0, r] = f[1]
            feat[1, r] = f[2]
            feat[2, r] = product
            feat[3, r] = gm
            lows[r] = product.astype(BF16)
            lows[rg] = gm.astype(BF16)

    def spectra(self, slot):
        lows, hat = self.slots[slot][5:]
        low = lows[...]
        hat[...] = mm(jnp.concatenate([low, low], axis=1), self.fwd[...])

    def filter(self, slot):
        _, coef_at, _, _, _, _, hat = self.slots[slot]
        spec, red = self.spec, self.red
        for k in range(self.ng):
            r = slice(GROUP * k, GROUP * (k + 1))
            rg = slice(SUB + GROUP * k, SUB + GROUP * (k + 1))
            ca, cb, cc = (row(coef_at, i, slice(k, k + 1)) for i in range(3))
            pr, pi = hat[r, :LANES], hat[r, LANES:]
            gr, gi = hat[rg, :LANES], hat[rg, LANES:]
            spec[r, :LANES] = (pr * ca - pi * cb).astype(BF16)
            spec[r, LANES:] = (pr * cb + pi * cc).astype(BF16)
            spec[rg, :LANES] = (gr * ca + gi * cb).astype(BF16)
            spec[rg, LANES:] = (gi * cc - gr * cb).astype(BF16)
            for i, value in enumerate((pr * gr, pi * gi, pr * gi - pi * gr)):
                red[i, 8 * k : 8 * k + 8, :] = value[:8] + value[8:]

    def invert(self):
        both = self.spec[...]
        self.res[...] = mm(jnp.concatenate([both, both], axis=1), self.inv[...])

    def gradients(self, block, slot):
        taps_at, _, skip_at, xs, feat, _, _ = self.slots[slot]
        own = own_channel()
        for k in range(self.ng):
            r = slice(GROUP * k, GROUP * (k + 1))
            rg = slice(SUB + GROUP * k, SUB + GROUP * (k + 1))
            cot = self.cot[pl.ds(self.rows(block) + GROUP * k, GROUP), :].astype(F32)
            kf, vf, product, gm = (feat[i, r] for i in range(4))
            sk = skip_at[r]
            gq = cot * (self.res[r] + sk * product)
            gp = self.res[rg] + sk * gm
            gf = [gq, gp * vf, gp * kf]
            self.sums[r] = (gm * product).astype(BF16)
            gfb = jnp.concatenate([g.astype(BF16) for g in gf], axis=0)
            xsb = jnp.concatenate(
                [xs[r, LANES * j : LANES * (j + 1)].astype(BF16) for j in range(self.taps)]
                + [jnp.zeros((GROUP, LANES), BF16)] * (LANES // GROUP - self.taps),
                axis=0,
            )
            corr = nt(gfb, xsb)
            if not self.last:
                for j in range(self.taps):
                    total = None
                    for m in range(3):
                        tap = row(taps_at, m * self.taps + j, slice(k, k + 1))
                        total = tap * gf[m] if total is None else total + tap * gf[m]
                    self.hats[r, LANES * j : LANES * (j + 1)] = total.astype(BF16)
            for m in range(3):
                kept = jnp.where(own, corr[GROUP * m : GROUP * (m + 1)], 0.0)
                self.red[3 + m, 8 * k : 8 * k + 8, :] = kept[:8] + kept[8:]

    def reduce(self, block, terms):
        for i in terms:
            total = self.red[i, pl.ds(0, self.ng, stride=8), :]
            for s in range(1, 8):
                total = total + self.red[i, pl.ds(s, self.ng, stride=8), :]
            self.acc[i, self.groups(block), :] = total

    def finish(self, block):
        if not self.last:
            rows = pl.ds(self.rows(block), SUB)
            gin = mm(self.hats[...], self.unshift[...]) + self.cot[rows, :].astype(F32)
            self.gin[rows, :] = gin.astype(BF16)
        self.skips[pl.ds(block, 1), :] = nt(jnp.ones((8, LANES), BF16), self.sums[...])[:1]
        self.reduce(block, range(3, 6))

    def step(self, block, blocks, slot):
        after = jnp.minimum(block + 1, blocks - 1)
        self.start(after, 1 - slot)
        self.filter(slot)
        self.invert()
        self.finish(jnp.maximum(block - 1, 0))
        self.features(after, 1 - slot)
        self.reduce(block, range(3))
        self.spectra(1 - slot)
        self.gradients(block, slot)

    def message(self):
        first = lax.broadcasted_iota(jnp.int32, (1, LANES), 1) == 0
        total = [self.acc[i] + self.acc_in[i] for i in range(6)]
        real = total[0] + jnp.where(first, 0.0, total[1])
        imag = jnp.where(first, total[1], total[2])
        both = jnp.concatenate([real, imag], axis=1)
        pick = (
            lax.broadcasted_iota(jnp.int32, (8, LANES), 1) // GROUP
            == lax.broadcasted_iota(jnp.int32, (8, LANES), 0)
        ).astype(F32)
        pieces = [mm(both, self.finv[...], PRECISE), self.skips[...] + self.skip_in[...]]
        pieces += [nt(pick, total[3 + m], PRECISE) for m in range(3)]
        pieces.append(jnp.zeros((8, LANES), F32))
        mine = jnp.concatenate(pieces, axis=0).astype(BF16)
        at = 0
        for ref in self.earlier:
            self.msg[: ref.shape[0]] = ref[...]
            at = ref.shape[0]
        self.msg[at : at + mine.shape[0]] = mine


def tick_kernel(last, taps, counts, *refs):
    ins, outs, scratch = refs[: counts[0]], refs[counts[0] : sum(counts)], refs[sum(counts) :]
    tick = Tick(last, taps, ins, outs, scratch)
    blocks = tick.x.shape[-2] // SUB
    tick.setup()
    tick.start(0, 0)
    tick.features(0, 0)
    tick.spectra(0)

    def pair(index, _):
        tick.step(2 * index, blocks, 0)
        tick.step(2 * index + 1, blocks, 1)
        return 0

    lax.fori_loop(0, blocks // 2, pair, 0)
    tick.finish(blocks - 1)
    if last:
        tick.message()


def in_hbm(array):
    return pltpu.with_memory_space_constraint(array, pltpu.HBM)


def run_tick(saved, cot, filters, medium, skip_rows, tick, chunk, chunks, prior):
    last = prior is not None
    total, length = saved.shape[-2:]
    channels = total // chunks
    taps = filters.shape[1]
    groups = channels // GROUP
    forward, inverse, inverse_full, shift, unshift = tables(length, taps)
    ng = SUB // GROUP
    full = lambda a: pl.BlockSpec(a.shape, lambda i: (0,) * len(a.shape))
    at = chunk if cot.shape[0] == total else 0
    ins = [saved, cot, filters, medium, skip_rows, forward, inverse, shift]
    ins += [inverse_full] if last else [unshift]
    ins = [a if last and a is cot else in_hbm(jnp.asarray(a)) for a in ins]
    ins += [*prior] if last else []
    in_specs = [
        pl.BlockSpec((1, 1, 1, channels, length), lambda i: (0, tick, 0, chunk, 0)),
        pl.BlockSpec((channels, length), lambda i: (at, 0)),
        pl.BlockSpec((3, taps, 1, groups), lambda i: (0, 0, 0, chunk)),
        pl.BlockSpec((1, groups, length), lambda i: (0, chunk, 0)),
        pl.BlockSpec((channels // LANES, LANES), lambda i: (chunk, 0)),
    ] + [full(a) for a in ins[5:]]
    acc_shape = (6, groups, LANES)
    skip_shape = (channels // LANES, LANES)
    slot = [
        pltpu.VMEM((3 * taps, ng, LANES), F32),
        pltpu.VMEM((3, ng, LANES), F32),
        pltpu.VMEM((SUB, LANES), F32),
        pltpu.VMEM((SUB, taps * LANES), F32),
        pltpu.VMEM((4, SUB, LANES), F32),
        pltpu.VMEM((2 * SUB, LANES), BF16),
        pltpu.VMEM((2 * SUB, 2 * LANES), F32),
    ]
    scratch = [pltpu.VMEM((groups, LANES), F32), pltpu.VMEM((3, groups, LANES), F32)]
    scratch += slot + slot
    scratch += [
        pltpu.VMEM((2 * SUB, 2 * LANES), BF16),
        pltpu.VMEM((2 * SUB, LANES), F32),
        pltpu.VMEM((6, 8 * ng, LANES), F32),
        pltpu.VMEM((SUB, LANES), BF16),
        pltpu.VMEM((SUB, taps * LANES), BF16),
        pltpu.VMEM((LANES, LANES), F32),
    ]
    if last:
        rows = (groups + channels // LANES + 32) * (chunk + 1)
        outs = [jax.ShapeDtypeStruct((rows, LANES), BF16)]
        scratch += [pltpu.VMEM(acc_shape, F32), pltpu.VMEM(skip_shape, F32)]
    else:
        outs = [
            jax.ShapeDtypeStruct((channels, length), BF16),
            jax.ShapeDtypeStruct(acc_shape, F32),
            jax.ShapeDtypeStruct(skip_shape, F32),
        ]
    return pl.pallas_call(
        functools.partial(tick_kernel, last, taps, (len(ins), len(outs))),
        out_shape=outs,
        grid=(1,),
        in_specs=in_specs,
        out_specs=[full(a) for a in outs],
        scratch_shapes=scratch,
        compiler_params=pltpu.CompilerParams(vmem_limit_bytes=48 << 20),
        name="last_tick" if last else "first_tick",
    )(*ins)


def finish_kernel(count, taps, chunks, *refs):
    ins, (short_ref, medium_ref, skip_ref) = refs[:count], refs[count:]
    total = ins[0][...].astype(F32)
    for ref in ins[1:]:
        total = total + ref[...].astype(F32)
    total = total * (1.0 / count)
    groups = medium_ref.shape[0] // chunks
    skips = skip_ref.shape[0] // chunks
    for c in range(chunks):
        at = c * (total.shape[0] // chunks)
        medium_ref[groups * c : groups * (c + 1)] = total[at : at + groups]
        at += groups
        skip_ref[skips * c : skips * (c + 1)] = total[at : at + skips]
        at += skips
        for m in range(3):
            for j in range(taps):
                short_ref[m, j, :, groups * c : groups * (c + 1)] = total[at + j : at + j + 1]
            at += 8


def finish(parts, groups, channels, taps, chunks):
    full = lambda a: pl.BlockSpec(a.shape, lambda i: (0,) * len(a.shape))
    outs = (
        jax.ShapeDtypeStruct((3, taps, 1, groups), F32),
        jax.ShapeDtypeStruct((groups, LANES), F32),
        jax.ShapeDtypeStruct((channels // LANES, LANES), F32),
    )
    return pl.pallas_call(
        functools.partial(finish_kernel, len(parts), taps, chunks),
        out_shape=outs,
        grid=(1,),
        in_specs=[full(a) for a in parts],
        out_specs=tuple(full(a) for a in outs),
        compiler_params=pltpu.CompilerParams(vmem_limit_bytes=8 << 20),
        name="finish",
    )(*parts)


def body(saved, upstream, short_filters, medium_filter, skip):
    channels = saved.shape[-2]
    groups, taps = short_filters.shape[2:]
    replicas = lax.axis_size("replica")
    chunks = groups // LANES
    skip_rows = skip.reshape(channels // LANES, LANES)
    filters = jnp.transpose(short_filters, (1, 3, 0, 2))
    rest = (filters, medium_filter, skip_rows)
    incoming, prior = [], []
    for c in range(chunks):
        gin, *sums = run_tick(saved, upstream[0, 0], *rest, 0, c, chunks, None)
        incoming.append(shifted(gin, "section", -1))
        prior.append(sums)
    message = []
    for c in range(chunks):
        message = run_tick(saved, incoming[c], *rest, 1, c, chunks, (*prior[c], *message))
    parts = [*message] + [
        lax.ppermute(message[0], "replica", [(i, (i + by) % replicas) for i in range(replicas)])
        for by in range(1, replicas)
    ]
    short, medium, skip_grad = finish(parts, groups, channels, taps, chunks)
    return (
        jnp.transpose(short, (2, 0, 3, 1)),
        medium[None],
        skip_grad.reshape(1, channels),
    )


def solution(mesh):
    placed = (
        P("section", None, "replica", None, None),
        P("section", "replica", None, None),
        P("section", None, None, None),
        P("section", None, None),
        P("section", None),
    )
    return jax.shard_map(
        body,
        mesh=mesh,
        in_specs=placed,
        out_specs=(P("section", None, None, None), P("section", None, None), P("section", None)),
        check_vma=False,
    )
```

```python
import functools

import jax
import jax.numpy as jnp
import numpy as np
from jax import lax
from jax.experimental import pallas as pl
from jax.experimental.pallas import tpu as pltpu
from jax.sharding import PartitionSpec as P

GROUP = 16
LANES = 128
SUB = 128
RING = 4

F32 = jnp.float32
BF16 = jnp.bfloat16
PRECISE = lax.Precision.HIGHEST


def shifted(array, axis, by):
    count = lax.axis_size(axis)
    pairs = [(i, i + by) for i in range(count) if 0 <= i + by < count]
    return lax.ppermute(array, axis, pairs)


def split(matrix):
    high = matrix.astype(jnp.bfloat16)
    low = (matrix - high.astype(np.float64)).astype(jnp.bfloat16)
    return high, low


@functools.lru_cache(None)
def tables(length, taps):
    points = 2 * length
    pos = np.arange(length)[:, None]
    freq = np.arange(length)[None, :]
    angle = 2.0 * np.pi * ((pos * freq) % points) / points
    real, imag = np.cos(angle), -np.sin(angle)
    imag[:, 0] = 1.0 - 2.0 * (np.arange(length) % 2)
    forward = np.concatenate([real, imag], axis=1)
    weight = np.full((2 * length, 1), 2.0 / points)
    weight[0] = weight[length] = 1.0 / points
    inverse = weight * forward.T
    shift = np.concatenate([np.eye(length, k=lag) for lag in range(1, taps)], axis=1)
    unshift = np.concatenate([np.eye(length, k=-lag) for lag in range(taps)], axis=0)
    return (
        np.concatenate(split(forward), axis=0),
        np.concatenate(split(inverse), axis=0),
        inverse.astype(np.float32),
        shift.astype(jnp.bfloat16),
        unshift.astype(jnp.bfloat16),
    )


def nt(left, right, precision=None):
    return lax.dot_general(
        left, right, (((1,), (1,)), ((), ())), precision=precision, preferred_element_type=F32
    )


def mm(left, right, precision=None):
    return jnp.dot(left, right, precision=precision, preferred_element_type=F32)


def row(ref, *index):
    return jnp.broadcast_to(ref[index], (GROUP, LANES))


def own_channel():
    lane = lax.broadcasted_iota(jnp.int32, (GROUP, LANES), 1)
    return lax.rem(lane, GROUP) == lax.broadcasted_iota(jnp.int32, (GROUP, LANES), 0)


class Tick:
    def __init__(self, last, taps, ins, outs, scratch):
        self.last, self.taps, self.ng = last, taps, SUB // GROUP
        (self.x, self.cot, self.f, self.med, self.skip, self.fwd, self.inv, self.shift) = ins[:8]
        scratch = list(scratch)
        if last:
            self.finv, self.acc_in, self.skip_in, *self.earlier = ins[8:]
            (self.msg,) = outs
            self.acc, self.skips = scratch.pop(0), scratch.pop(0)
        else:
            (self.unshift,) = ins[8:]
            self.gin, self.acc, self.skips = outs
        self.columns, self.coef, self.turn = scratch[:3]
        rings = [scratch[i : i + RING] for i in range(3, len(scratch), RING)]
        (self.taps_at, self.coef_at, self.skip_at, self.xs, self.feat, self.lows, self.hat,
         self.spec, self.res, self.terms, self.sums, self.hats, self.corr) = rings

    def rows(self, block):
        return pl.multiple_of(block * SUB, SUB)

    def groups(self, block):
        return pl.ds(pl.multiple_of(block * self.ng, self.ng), self.ng)

    def setup(self):
        first = lax.broadcasted_iota(jnp.int32, (1, LANES), 1) == 0
        h = self.med[0].astype(BF16)
        hh = mm(jnp.concatenate([h, h], axis=1), self.fwd[...])
        hr, hi = hh[:, :LANES], hh[:, LANES:]
        self.coef[0] = hr
        self.coef[1] = jnp.where(first, 0.0, hi)
        self.coef[2] = jnp.where(first, hi, hr)
        self.turn[...] = jnp.zeros_like(self.turn)
        for q in range(h.shape[0] // LANES):
            cols = slice(LANES * q, LANES * (q + 1))
            for m in range(3):
                for j in range(self.taps):
                    t = m * self.taps + j
                    self.turn[t : t + 1, :] = self.f[m, j, :, cols]
            self.columns[cols, :] = self.turn[...].T

    def start(self, block, slot):
        taps_at, skip_at, xs = self.taps_at[slot], self.skip_at[slot], self.xs[slot]
        x = self.x[0, 0, 0, pl.ds(self.rows(block), SUB), :]
        xs[:, LANES:] = mm(x, self.shift[...])
        xs[:, :LANES] = x.astype(F32)
        mine = self.columns[self.groups(block), :]
        for t in range(3 * self.taps):
            taps_at[t] = jnp.broadcast_to(mine[:, t : t + 1], (self.ng, LANES))
        for i in range(3):
            self.coef_at[slot][i] = self.coef[i, self.groups(block), :]
        for q in range(SUB // LANES):
            skip = self.skip[pl.ds(block * (SUB // LANES) + q, 1), :]
            skip_at[LANES * q : LANES * (q + 1)] = jnp.broadcast_to(skip, (LANES, LANES)).T

    def features(self, block, slot):
        taps_at, xs, feat, lows = (r[slot] for r in (self.taps_at, self.xs, self.feat, self.lows))
        for k in range(self.ng):
            r = slice(GROUP * k, GROUP * (k + 1))
            rg = slice(SUB + GROUP * k, SUB + GROUP * (k + 1))
            f = []
            for m in range(3):
                total = None
                for j in range(self.taps):
                    tap = row(taps_at, m * self.taps + j, slice(k, k + 1))
                    term = tap * xs[r, LANES * j : LANES * (j + 1)]
                    total = term if total is None else total + term
                f.append(total)
            product = f[1] * f[2]
            gm = self.cot[pl.ds(self.rows(block) + GROUP * k, GROUP), :].astype(F32) * f[0]
            feat[0, r] = f[1]
            feat[1, r] = f[2]
            feat[2, r] = product
            feat[3, r] = gm
            lows[r] = product.astype(BF16)
            lows[rg] = gm.astype(BF16)
        low = lows[...]
        self.hat[slot][...] = mm(jnp.concatenate([low, low], axis=1), self.fwd[...])

    def filter(self, slot):
        coef_at, hat, spec, terms = (
            r[slot] for r in (self.coef_at, self.hat, self.spec, self.terms)
        )
        for k in range(self.ng):
            r = slice(GROUP * k, GROUP * (k + 1))
            rg = slice(SUB + GROUP * k, SUB + GROUP * (k + 1))
            ca, cb, cc = (row(coef_at, i, slice(k, k + 1)) for i in range(3))
            pr, pi = hat[r, :LANES], hat[r, LANES:]
            gr, gi = hat[rg, :LANES], hat[rg, LANES:]
            spec[r, :LANES] = (pr * ca - pi * cb).astype(BF16)
            spec[r, LANES:] = (pr * cb + pi * cc).astype(BF16)
            spec[rg, :LANES] = (gr * ca + gi * cb).astype(BF16)
            spec[rg, LANES:] = (gi * cc - gr * cb).astype(BF16)
            for i, value in enumerate((pr * gr, pi * gi, pr * gi - pi * gr)):
                terms[i, 8 * k : 8 * k + 8, :] = value[:8] + value[8:]
        both = spec[...]
        self.res[slot][...] = mm(jnp.concatenate([both, both], axis=1), self.inv[...])

    def gradients(self, block, slot):
        taps_at, skip_at, xs, feat, res, sums, hats, corr = (
            r[slot]
            for r in (self.taps_at, self.skip_at, self.xs, self.feat, self.res, self.sums,
                      self.hats, self.corr)
        )
        for k in range(self.ng):
            r = slice(GROUP * k, GROUP * (k + 1))
            rg = slice(SUB + GROUP * k, SUB + GROUP * (k + 1))
            cot = self.cot[pl.ds(self.rows(block) + GROUP * k, GROUP), :].astype(F32)
            kf, vf, product, gm = (feat[i, r] for i in range(4))
            sk = skip_at[r]
            gq = cot * (res[r] + sk * product)
            gp = res[rg] + sk * gm
            gf = [gq, gp * vf, gp * kf]
            sums[r] = (gm * product).astype(BF16)
            gfb = jnp.concatenate([g.astype(BF16) for g in gf], axis=0)
            xsb = jnp.concatenate(
                [xs[r, LANES * j : LANES * (j + 1)].astype(BF16) for j in range(self.taps)]
                + [jnp.zeros((GROUP, LANES), BF16)] * (LANES // GROUP - self.taps),
                axis=0,
            )
            corr[k] = nt(gfb, xsb)
            if not self.last:
                for j in range(self.taps):
                    total = None
                    for m in range(3):
                        tap = row(taps_at, m * self.taps + j, slice(k, k + 1))
                        total = tap * gf[m] if total is None else total + tap * gf[m]
                    hats[r, LANES * j : LANES * (j + 1)] = total.astype(BF16)

    def finish(self, block, slot):
        terms, corr = self.terms[slot], self.corr[slot]
        own = own_channel()
        for k in range(self.ng):
            for m in range(3):
                kept = jnp.where(own, corr[k, GROUP * m : GROUP * (m + 1)], 0.0)
                terms[3 + m, 8 * k : 8 * k + 8, :] = kept[:8] + kept[8:]
        for i in range(6):
            total = terms[i, pl.ds(0, self.ng, stride=8), :]
            for s in range(1, 8):
                total = total + terms[i, pl.ds(s, self.ng, stride=8), :]
            self.acc[i, self.groups(block), :] = total
        if not self.last:
            rows = pl.ds(self.rows(block), SUB)
            gin = mm(self.hats[slot][...], self.unshift[...]) + self.cot[rows, :].astype(F32)
            self.gin[rows, :] = gin.astype(BF16)
        sums = nt(jnp.ones((8, LANES), BF16), self.sums[slot][...])
        for q in range(SUB // LANES):
            at = pl.ds(block * (SUB // LANES) + q, 1)
            self.skips[at, :] = sums[:1, LANES * q : LANES * (q + 1)]

    def run(self, blocks):
        for t in range(3):
            self.start(t, t % RING)
        for t in range(2):
            self.features(t, t % RING)
        self.filter(0)

        def turn(index, _):
            for u in range(RING):
                t = RING * index + u
                stages = {
                    "a": (self.start, jnp.minimum(t + 3, blocks - 1), (u + 3) % RING),
                    "b": (self.features, jnp.minimum(t + 2, blocks - 1), (u + 2) % RING),
                    "c": (self.filter, (u + 1) % RING),
                    "d": (self.gradients, t, u),
                    "e": (self.finish, jnp.maximum(t - 1, 0), (u - 1) % RING),
                }
                for name in "aecbd" if self.last else "cadbe":
                    stage, *where = stages[name]
                    stage(*where)
            return 0

        lax.fori_loop(0, blocks // RING, turn, 0)
        self.finish(blocks - 1, (blocks - 1) % RING)

    def message(self):
        first = lax.broadcasted_iota(jnp.int32, (1, LANES), 1) == 0
        total = [self.acc[i] + self.acc_in[i] for i in range(6)]
        real = total[0] + jnp.where(first, 0.0, total[1])
        imag = jnp.where(first, total[1], total[2])
        both = jnp.concatenate([real, imag], axis=1)
        pick = (
            lax.broadcasted_iota(jnp.int32, (8, LANES), 1) // GROUP
            == lax.broadcasted_iota(jnp.int32, (8, LANES), 0)
        ).astype(F32)
        pieces = [mm(both, self.finv[...], PRECISE), self.skips[...] + self.skip_in[...]]
        pieces += [nt(pick, total[3 + m], PRECISE) for m in range(3)]
        pieces.append(jnp.zeros((8, LANES), F32))
        mine = jnp.concatenate(pieces, axis=0).astype(BF16)
        at = 0
        for ref in self.earlier:
            self.msg[: ref.shape[0]] = ref[...]
            at = ref.shape[0]
        self.msg[at : at + mine.shape[0]] = mine


def tick_kernel(last, taps, counts, *refs):
    ins, outs, scratch = refs[: counts[0]], refs[counts[0] : sum(counts)], refs[sum(counts) :]
    tick = Tick(last, taps, ins, outs, scratch)
    blocks = tick.x.shape[-2] // SUB
    tick.setup()
    tick.run(blocks)
    if last:
        tick.message()


def in_hbm(array):
    return pltpu.with_memory_space_constraint(array, pltpu.HBM)


def run_tick(saved, cot, filters, medium, skip_rows, tick, chunk, chunks, prior):
    last = prior is not None
    total, length = saved.shape[-2:]
    channels = total // chunks
    taps = filters.shape[1]
    groups = channels // GROUP
    forward, inverse, inverse_full, shift, unshift = tables(length, taps)
    ng = SUB // GROUP
    full = lambda a: pl.BlockSpec(a.shape, lambda i: (0,) * len(a.shape))
    at = chunk if cot.shape[0] == total else 0
    ins = [saved, cot, filters, medium, skip_rows, forward, inverse, shift]
    ins += [inverse_full] if last else [unshift]
    if not last and chunk == 0:
        ins = [in_hbm(jnp.asarray(a)) for a in ins]
    ins += [*prior] if last else []
    in_specs = [
        pl.BlockSpec((1, 1, 1, channels, length), lambda i: (0, tick, 0, chunk, 0)),
        pl.BlockSpec((channels, length), lambda i: (at, 0)),
        pl.BlockSpec((3, taps, 1, groups), lambda i: (0, 0, 0, chunk)),
        pl.BlockSpec((1, groups, length), lambda i: (0, chunk, 0)),
        pl.BlockSpec((channels // LANES, LANES), lambda i: (chunk, 0)),
    ] + [full(a) for a in ins[5:]]
    acc_shape = (6, groups, LANES)
    skip_shape = (channels // LANES, LANES)
    ring = [
        pltpu.VMEM((3 * taps, ng, LANES), F32),
        pltpu.VMEM((3, ng, LANES), F32),
        pltpu.VMEM((SUB, LANES), F32),
        pltpu.VMEM((SUB, taps * LANES), F32),
        pltpu.VMEM((4, SUB, LANES), F32),
        pltpu.VMEM((2 * SUB, LANES), BF16),
        pltpu.VMEM((2 * SUB, 2 * LANES), F32),
        pltpu.VMEM((2 * SUB, 2 * LANES), BF16),
        pltpu.VMEM((2 * SUB, LANES), F32),
        pltpu.VMEM((6, 8 * ng, LANES), F32),
        pltpu.VMEM((SUB, LANES), BF16),
        pltpu.VMEM((SUB, taps * LANES), BF16),
        pltpu.VMEM((ng, 3 * GROUP, LANES), F32),
    ]
    scratch = [pltpu.VMEM(acc_shape, F32), pltpu.VMEM(skip_shape, F32)] if last else []
    scratch += [
        pltpu.VMEM((groups, LANES), F32),
        pltpu.VMEM((3, groups, LANES), F32),
        pltpu.VMEM((LANES, LANES), F32),
    ]
    scratch += [ref for ref in ring for _ in range(RING)]
    if last:
        rows = (groups + channels // LANES + 32) * (chunk + 1)
        outs = [jax.ShapeDtypeStruct((rows, LANES), BF16)]
    else:
        outs = [
            jax.ShapeDtypeStruct((channels, length), BF16),
            jax.ShapeDtypeStruct(acc_shape, F32),
            jax.ShapeDtypeStruct(skip_shape, F32),
        ]
    return pl.pallas_call(
        functools.partial(tick_kernel, last, taps, (len(ins), len(outs))),
        out_shape=outs,
        grid=(1,),
        in_specs=in_specs,
        out_specs=[full(a) for a in outs],
        scratch_shapes=scratch,
        compiler_params=pltpu.CompilerParams(vmem_limit_bytes=48 << 20),
        name="last_tick" if last else "first_tick",
    )(*ins)


def finish_kernel(count, taps, chunks, *refs):
    ins, (short_ref, medium_ref, skip_ref) = refs[:count], refs[count:]
    total = ins[0][...].astype(F32)
    for ref in ins[1:]:
        total = total + ref[...].astype(F32)
    total = total * (1.0 / count)
    groups = medium_ref.shape[0] // chunks
    skips = skip_ref.shape[0] // chunks
    for c in range(chunks):
        at = c * (total.shape[0] // chunks)
        medium_ref[groups * c : groups * (c + 1)] = total[at : at + groups]
        at += groups
        skip_ref[skips * c : skips * (c + 1)] = total[at : at + skips]
        at += skips
        for m in range(3):
            for j in range(taps):
                short_ref[m, j, :, groups * c : groups * (c + 1)] = total[at + j : at + j + 1]
            at += 8


def finish(parts, groups, channels, taps, chunks):
    full = lambda a: pl.BlockSpec(a.shape, lambda i: (0,) * len(a.shape))
    outs = (
        jax.ShapeDtypeStruct((3, taps, 1, groups), F32),
        jax.ShapeDtypeStruct((groups, LANES), F32),
        jax.ShapeDtypeStruct((channels // LANES, LANES), F32),
    )
    return pl.pallas_call(
        functools.partial(finish_kernel, len(parts), taps, chunks),
        out_shape=outs,
        grid=(1,),
        in_specs=[full(a) for a in parts],
        out_specs=tuple(full(a) for a in outs),
        compiler_params=pltpu.CompilerParams(vmem_limit_bytes=8 << 20),
        name="finish",
    )(*parts)


def body(saved, upstream, short_filters, medium_filter, skip):
    channels = saved.shape[-2]
    groups, taps = short_filters.shape[2:]
    replicas = lax.axis_size("replica")
    chunks = groups // LANES
    skip_rows = skip.reshape(channels // LANES, LANES)
    filters = jnp.transpose(short_filters, (1, 3, 0, 2))
    rest = (filters, medium_filter, skip_rows)
    incoming, prior = [], []
    for c in range(chunks):
        gin, *sums = run_tick(saved, upstream[0, 0], *rest, 0, c, chunks, None)
        incoming.append(shifted(gin, "section", -1))
        prior.append(sums)
    message = []
    for c in range(chunks):
        message = run_tick(saved, incoming[c], *rest, 1, c, chunks, (*prior[c], *message))
    parts = [*message] + [
        lax.ppermute(message[0], "replica", [(i, (i + by) % replicas) for i in range(replicas)])
        for by in range(1, replicas)
    ]
    short, medium, skip_grad = finish(parts, groups, channels, taps, chunks)
    return (
        jnp.transpose(short, (2, 0, 3, 1)),
        medium[None],
        skip_grad.reshape(1, channels),
    )


def solution(mesh):
    placed = (
        P("section", None, "replica", None, None),
        P("section", "replica", None, None),
        P("section", None, None, None),
        P("section", None, None),
        P("section", None),
    )
    return jax.shard_map(
        body,
        mesh=mesh,
        in_specs=placed,
        out_specs=(P("section", None, None, None), P("section", None, None), P("section", None)),
        check_vma=False,
    )
```

```python
import functools

import jax
import jax.numpy as jnp
import numpy as np
from jax import lax
from jax.experimental import pallas as pl
from jax.experimental.pallas import tpu as pltpu
from jax.sharding import PartitionSpec as P

GROUP = 16
LANES = 128
SUB = 128
RING = 4

F32 = jnp.float32
BF16 = jnp.bfloat16
PRECISE = lax.Precision.HIGHEST


def shifted(array, axis, by):
    count = lax.axis_size(axis)
    pairs = [(i, i + by) for i in range(count) if 0 <= i + by < count]
    return lax.ppermute(array, axis, pairs)


def split(matrix):
    high = matrix.astype(jnp.bfloat16)
    low = (matrix - high.astype(np.float64)).astype(jnp.bfloat16)
    return high, low


@functools.lru_cache(None)
def tables(length, taps):
    points = 2 * length
    pos = np.arange(length)[:, None]
    freq = np.arange(length)[None, :]
    angle = 2.0 * np.pi * ((pos * freq) % points) / points
    real, imag = np.cos(angle), -np.sin(angle)
    imag[:, 0] = 1.0 - 2.0 * (np.arange(length) % 2)
    forward = np.concatenate([real, imag], axis=1)
    weight = np.full((2 * length, 1), 2.0 / points)
    weight[0] = weight[length] = 1.0 / points
    inverse = weight * forward.T
    shift = np.concatenate([np.eye(length, k=lag) for lag in range(1, taps)], axis=1)
    unshift = np.concatenate([np.eye(length, k=-lag) for lag in range(taps)], axis=0)
    return (
        np.concatenate(split(forward), axis=0),
        np.concatenate(split(inverse), axis=1),
        inverse.astype(np.float32),
        shift.astype(jnp.bfloat16),
        unshift.astype(jnp.bfloat16),
    )


def nt(left, right, precision=None):
    return lax.dot_general(
        left, right, (((1,), (1,)), ((), ())), precision=precision, preferred_element_type=F32
    )


def mm(left, right, precision=None):
    return jnp.dot(left, right, precision=precision, preferred_element_type=F32)


def row(ref, *index):
    return jnp.broadcast_to(ref[index], (GROUP, LANES))


def own_channel():
    lane = lax.broadcasted_iota(jnp.int32, (GROUP, LANES), 1)
    return lax.rem(lane, GROUP) == lax.broadcasted_iota(jnp.int32, (GROUP, LANES), 0)


class Tick:
    def __init__(self, last, taps, ins, outs, scratch):
        self.last, self.taps, self.ng = last, taps, SUB // GROUP
        (self.x, self.cot, self.f, self.med, self.skip, self.fwd, self.inv, self.shift) = ins[:8]
        scratch = list(scratch)
        if last:
            self.finv, self.acc_in, self.skip_in, *self.earlier = ins[8:]
            (self.msg,) = outs
            self.acc, self.skips = scratch.pop(0), scratch.pop(0)
        else:
            (self.unshift,) = ins[8:]
            self.gin, self.acc, self.skips = outs
        self.columns, self.coef, self.turn = scratch[:3]
        rings = [scratch[i : i + RING] for i in range(3, len(scratch), RING)]
        (self.taps_at, self.coef_at, self.skip_at, self.xs, self.feat, self.lows, self.hat,
         self.spec, self.res, self.terms, self.sums, self.hats, self.corr) = rings

    def rows(self, block):
        return pl.multiple_of(block * SUB, SUB)

    def groups(self, block):
        return pl.ds(pl.multiple_of(block * self.ng, self.ng), self.ng)

    def setup(self):
        first = lax.broadcasted_iota(jnp.int32, (1, LANES), 1) == 0
        h = self.med[...].astype(BF16)
        hh = mm(jnp.concatenate([h, h], axis=1), self.fwd[...])
        hr, hi = hh[:, :LANES], hh[:, LANES:]
        self.coef[0] = hr
        self.coef[1] = jnp.where(first, 0.0, hi)
        self.coef[2] = jnp.where(first, hi, hr)
        self.turn[...] = jnp.zeros_like(self.turn)
        for q in range(h.shape[0] // LANES):
            cols = slice(LANES * q, LANES * (q + 1))
            for m in range(3):
                for j in range(self.taps):
                    t = m * self.taps + j
                    self.turn[t : t + 1, :] = self.f[m, j, :, cols]
            self.columns[cols, :] = self.turn[...].T

    def start(self, block, slot):
        taps_at, skip_at, xs = self.taps_at[slot], self.skip_at[slot], self.xs[slot]
        x = self.x[pl.ds(self.rows(block), SUB), :]
        xs[:, LANES:] = mm(x, self.shift[...])
        xs[:, :LANES] = x.astype(F32)
        mine = self.columns[self.groups(block), :]
        for t in range(3 * self.taps):
            taps_at[t] = jnp.broadcast_to(mine[:, t : t + 1], (self.ng, LANES))
        for i in range(3):
            self.coef_at[slot][i] = self.coef[i, self.groups(block), :]
        for q in range(SUB // LANES):
            skip = self.skip[pl.ds(block * (SUB // LANES) + q, 1), :]
            skip_at[LANES * q : LANES * (q + 1)] = jnp.broadcast_to(skip, (LANES, LANES)).T

    def features(self, block, slot):
        taps_at, xs, feat, lows = (r[slot] for r in (self.taps_at, self.xs, self.feat, self.lows))
        for k in range(self.ng):
            r = slice(GROUP * k, GROUP * (k + 1))
            rg = slice(SUB + GROUP * k, SUB + GROUP * (k + 1))
            f = []
            for m in range(3):
                total = None
                for j in range(self.taps):
                    tap = row(taps_at, m * self.taps + j, slice(k, k + 1))
                    term = tap * xs[r, LANES * j : LANES * (j + 1)]
                    total = term if total is None else total + term
                f.append(total)
            product = f[1] * f[2]
            gm = self.cot[pl.ds(self.rows(block) + GROUP * k, GROUP), :].astype(F32) * f[0]
            feat[0, r] = f[1]
            feat[1, r] = f[2]
            feat[2, r] = product
            feat[3, r] = gm
            lows[r] = product.astype(BF16)
            lows[rg] = gm.astype(BF16)
        low = lows[...]
        self.hat[slot][...] = mm(jnp.concatenate([low, low], axis=1), self.fwd[...])

    def filter(self, slot):
        coef_at, hat, spec, terms = (
            r[slot] for r in (self.coef_at, self.hat, self.spec, self.terms)
        )
        for k in range(self.ng):
            r = slice(GROUP * k, GROUP * (k + 1))
            rg = slice(SUB + GROUP * k, SUB + GROUP * (k + 1))
            ca, cb, cc = (row(coef_at, i, slice(k, k + 1)) for i in range(3))
            pr, pi = hat[r, :LANES], hat[r, LANES:]
            gr, gi = hat[rg, :LANES], hat[rg, LANES:]
            spec[r, :LANES] = (pr * ca - pi * cb).astype(BF16)
            spec[r, LANES:] = (pr * cb + pi * cc).astype(BF16)
            spec[rg, :LANES] = (gr * ca + gi * cb).astype(BF16)
            spec[rg, LANES:] = (gi * cc - gr * cb).astype(BF16)
            for i, value in enumerate((pr * gr, pi * gi, pr * gi - pi * gr)):
                terms[i, 8 * k : 8 * k + 8, :] = value[:8] + value[8:]
        wide = mm(spec[...], self.inv[...])
        self.res[slot][...] = wide[:, :LANES] + wide[:, LANES:]

    def gradients(self, block, slot):
        taps_at, skip_at, xs, feat, res, sums, hats, corr = (
            r[slot]
            for r in (self.taps_at, self.skip_at, self.xs, self.feat, self.res, self.sums,
                      self.hats, self.corr)
        )
        for k in range(self.ng):
            r = slice(GROUP * k, GROUP * (k + 1))
            rg = slice(SUB + GROUP * k, SUB + GROUP * (k + 1))
            cot = self.cot[pl.ds(self.rows(block) + GROUP * k, GROUP), :].astype(F32)
            kf, vf, product, gm = (feat[i, r] for i in range(4))
            sk = skip_at[r]
            gq = cot * (res[r] + sk * product)
            gp = res[rg] + sk * gm
            gf = [gq, gp * vf, gp * kf]
            sums[r] = (gm * product).astype(BF16)
            gfb = jnp.concatenate([g.astype(BF16) for g in gf], axis=0)
            xsb = jnp.concatenate(
                [self.x[pl.ds(self.rows(block) + GROUP * k, GROUP), :]]
                + [xs[r, LANES * j : LANES * (j + 1)].astype(BF16) for j in range(1, self.taps)]
                + [jnp.zeros((GROUP, LANES), BF16)] * (LANES // GROUP - self.taps),
                axis=0,
            )
            corr[k] = nt(gfb, xsb)
            if not self.last:
                for j in range(self.taps):
                    total = None
                    for m in range(3):
                        tap = row(taps_at, m * self.taps + j, slice(k, k + 1))
                        total = tap * gf[m] if total is None else total + tap * gf[m]
                    hats[r, LANES * j : LANES * (j + 1)] = total.astype(BF16)

    def finish(self, block, slot):
        terms, corr = self.terms[slot], self.corr[slot]
        own = own_channel()
        for k in range(self.ng):
            for m in range(3):
                kept = jnp.where(own, corr[k, GROUP * m : GROUP * (m + 1)], 0.0)
                terms[3 + m, 8 * k : 8 * k + 8, :] = kept[:8] + kept[8:]
        for i in range(6):
            total = terms[i, pl.ds(0, self.ng, stride=8), :]
            for s in range(1, 8):
                total = total + terms[i, pl.ds(s, self.ng, stride=8), :]
            self.acc[i, self.groups(block), :] = total
        if not self.last:
            rows = pl.ds(self.rows(block), SUB)
            gin = mm(self.hats[slot][...], self.unshift[...]) + self.cot[rows, :].astype(F32)
            self.gin[rows, :] = gin.astype(BF16)
        sums = nt(jnp.ones((8, LANES), BF16), self.sums[slot][...])
        for q in range(SUB // LANES):
            at = pl.ds(block * (SUB // LANES) + q, 1)
            self.skips[at, :] = sums[:1, LANES * q : LANES * (q + 1)]

    def run(self, blocks):
        for t in range(3):
            self.start(t, t % RING)
        for t in range(2):
            self.features(t, t % RING)
        self.filter(0)

        order = "aecbd" if self.last else "cadbe"

        def step(t, u, left):
            stages = {
                "a": (3, self.start, t + 3, (u + 3) % RING),
                "b": (2, self.features, t + 2, (u + 2) % RING),
                "c": (1, self.filter, (u + 1) % RING),
                "d": (0, self.gradients, t, u),
                "e": (0, self.finish, jnp.maximum(t - 1, 0), (u - 1) % RING),
            }
            for name in order:
                ahead, stage, *where = stages[name]
                if ahead < left:
                    stage(*where)

        def turn(index, _):
            for u in range(RING):
                step(RING * index + u, u, RING)
            return 0

        lax.fori_loop(0, blocks // RING - 1, turn, 0)
        for u in range(RING):
            step(blocks - RING + u, u, RING - u)
        self.finish(blocks - 1, (blocks - 1) % RING)

    def message(self):
        first = lax.broadcasted_iota(jnp.int32, (1, LANES), 1) == 0
        total = [self.acc[i] + self.acc_in[i] for i in range(6)]
        real = total[0] + jnp.where(first, 0.0, total[1])
        imag = jnp.where(first, total[1], total[2])
        both = jnp.concatenate([real, imag], axis=1)
        pick = (
            lax.broadcasted_iota(jnp.int32, (8, LANES), 1) // GROUP
            == lax.broadcasted_iota(jnp.int32, (8, LANES), 0)
        ).astype(F32)
        pieces = [mm(both, self.finv[...], PRECISE), self.skips[...] + self.skip_in[...]]
        pieces += [nt(pick, total[3 + m], PRECISE) for m in range(3)]
        pieces.append(jnp.zeros((8, LANES), F32))
        mine = jnp.concatenate(pieces, axis=0).astype(BF16)
        at = 0
        for ref in self.earlier:
            self.msg[: ref.shape[0]] = ref[...]
            at = ref.shape[0]
        self.msg[at : at + mine.shape[0]] = mine


def tick_kernel(last, taps, counts, where, *refs):
    ins, outs, scratch = refs[: counts[0]], refs[counts[0] : sum(counts)], refs[sum(counts) :]
    x, cot, f, med, skip = ins[:5]
    tick, chunk, at, channels = where
    if chunk is None:
        views = (x.at[0, 0, 0], cot, f, med.at[0], skip)
    else:
        groups, rows = channels // GROUP, channels // LANES
        views = (
            x.at[0, tick, 0, pl.ds(chunk * channels, channels), :],
            cot.at[pl.ds(at * channels, channels), :],
            f.at[:, :, :, pl.ds(chunk * groups, groups)],
            med.at[0, pl.ds(chunk * groups, groups), :],
            skip.at[pl.ds(chunk * rows, rows), :],
        )
    work = Tick(last, taps, (*views, *ins[5:]), outs, scratch)
    work.setup()
    work.run(channels // SUB)
    if last:
        work.message()


def in_hbm(array):
    return pltpu.with_memory_space_constraint(array, pltpu.HBM)


def run_tick(saved, cot, filters, medium, skip_rows, tick, chunk, chunks, prior):
    last = prior is not None
    total, length = saved.shape[-2:]
    channels = total // chunks
    taps = filters.shape[1]
    groups = channels // GROUP
    forward, inverse, inverse_full, shift, unshift = tables(length, taps)
    ng = SUB // GROUP
    full = lambda a: pl.BlockSpec(a.shape, lambda i: (0,) * len(a.shape))
    at = chunk if cot.shape[0] == total else 0
    ins = [saved, cot, filters, medium, skip_rows, forward, inverse, shift]
    ins += [inverse_full] if last else [unshift]
    fetch = not last and chunk == 0
    if fetch:
        ins = [in_hbm(jnp.asarray(a)) for a in ins]
    ins += [*prior] if last else []
    in_specs = [
        pl.BlockSpec((1, 1, 1, channels, length), lambda i: (0, tick, 0, chunk, 0)),
        pl.BlockSpec((channels, length), lambda i: (at, 0)),
        pl.BlockSpec((3, taps, 1, groups), lambda i: (0, 0, 0, chunk)),
        pl.BlockSpec((1, groups, length), lambda i: (0, chunk, 0)),
        pl.BlockSpec((channels // LANES, LANES), lambda i: (chunk, 0)),
    ] + [full(a) for a in ins[5:]]
    whole = pl.BlockSpec(memory_space=pltpu.VMEM)
    if not fetch:
        in_specs = [whole] * len(ins)
    acc_shape = (6, groups, LANES)
    skip_shape = (channels // LANES, LANES)
    ring = [
        pltpu.VMEM((3 * taps, ng, LANES), F32),
        pltpu.VMEM((3, ng, LANES), F32),
        pltpu.VMEM((SUB, LANES), F32),
        pltpu.VMEM((SUB, taps * LANES), F32),
        pltpu.VMEM((4, SUB, LANES), F32),
        pltpu.VMEM((2 * SUB, LANES), BF16),
        pltpu.VMEM((2 * SUB, 2 * LANES), F32),
        pltpu.VMEM((2 * SUB, 2 * LANES), BF16),
        pltpu.VMEM((2 * SUB, LANES), F32),
        pltpu.VMEM((6, 8 * ng, LANES), F32),
        pltpu.VMEM((SUB, LANES), BF16),
        pltpu.VMEM((SUB, taps * LANES), BF16),
        pltpu.VMEM((ng, 3 * GROUP, LANES), F32),
    ]
    scratch = [pltpu.VMEM(acc_shape, F32), pltpu.VMEM(skip_shape, F32)] if last else []
    scratch += [
        pltpu.VMEM((groups, LANES), F32),
        pltpu.VMEM((3, groups, LANES), F32),
        pltpu.VMEM((LANES, LANES), F32),
    ]
    scratch += [ref for ref in ring for _ in range(RING)]
    if last:
        rows = (groups + channels // LANES + 32) * (chunk + 1)
        outs = [jax.ShapeDtypeStruct((rows, LANES), BF16)]
    else:
        outs = [
            jax.ShapeDtypeStruct((channels, length), BF16),
            jax.ShapeDtypeStruct(acc_shape, F32),
            jax.ShapeDtypeStruct(skip_shape, F32),
        ]
    return pl.pallas_call(
        functools.partial(
            tick_kernel, last, taps, (len(ins), len(outs)),
            (tick, None if fetch else chunk, at, channels),
        ),
        out_shape=outs,
        grid=(1,),
        in_specs=in_specs,
        out_specs=[whole] * len(outs),
        scratch_shapes=scratch,
        compiler_params=pltpu.CompilerParams(vmem_limit_bytes=48 << 20),
        name="last_tick" if last else "first_tick",
    )(*ins)


def finish_kernel(count, taps, chunks, *refs):
    ins, (short_ref, medium_ref, skip_ref) = refs[:count], refs[count:]
    total = ins[0][...].astype(F32)
    for ref in ins[1:]:
        total = total + ref[...].astype(F32)
    total = total * (1.0 / count)
    groups = medium_ref.shape[0] // chunks
    skips = skip_ref.shape[0] // chunks
    for c in range(chunks):
        at = c * (total.shape[0] // chunks)
        medium_ref[groups * c : groups * (c + 1)] = total[at : at + groups]
        at += groups
        skip_ref[skips * c : skips * (c + 1)] = total[at : at + skips]
        at += skips
        for m in range(3):
            for j in range(taps):
                short_ref[m, j, :, groups * c : groups * (c + 1)] = total[at + j : at + j + 1]
            at += 8


def finish(parts, groups, channels, taps, chunks):
    full = lambda a: pl.BlockSpec(a.shape, lambda i: (0,) * len(a.shape))
    outs = (
        jax.ShapeDtypeStruct((3, taps, 1, groups), F32),
        jax.ShapeDtypeStruct((groups, LANES), F32),
        jax.ShapeDtypeStruct((channels // LANES, LANES), F32),
    )
    return pl.pallas_call(
        functools.partial(finish_kernel, len(parts), taps, chunks),
        out_shape=outs,
        grid=(1,),
        in_specs=[full(a) for a in parts],
        out_specs=tuple(full(a) for a in outs),
        compiler_params=pltpu.CompilerParams(vmem_limit_bytes=8 << 20),
        name="finish",
    )(*parts)


def body(saved, upstream, short_filters, medium_filter, skip):
    channels = saved.shape[-2]
    groups, taps = short_filters.shape[2:]
    replicas = lax.axis_size("replica")
    chunks = groups // LANES
    skip_rows = skip.reshape(channels // LANES, LANES)
    filters = jnp.transpose(short_filters, (1, 3, 0, 2))
    rest = (filters, medium_filter, skip_rows)
    incoming, prior = [], []
    for c in range(chunks):
        gin, *sums = run_tick(saved, upstream[0, 0], *rest, 0, c, chunks, None)
        incoming.append(shifted(gin, "section", -1))
        prior.append(sums)
    message = []
    for c in range(chunks):
        message = run_tick(saved, incoming[c], *rest, 1, c, chunks, (*prior[c], *message))
    even = replicas & (replicas - 1) == 0
    parts = [*message]
    for by in range(1, replicas):
        pairs = [(i, i ^ by if even else (i + by) % replicas) for i in range(replicas)]
        parts.append(lax.ppermute(message[0], "replica", pairs))
    short, medium, skip_grad = finish(parts, groups, channels, taps, chunks)
    return (
        jnp.transpose(short, (2, 0, 3, 1)),
        medium[None],
        skip_grad.reshape(1, channels),
    )


def solution(mesh):
    placed = (
        P("section", None, "replica", None, None),
        P("section", "replica", None, None),
        P("section", None, None, None),
        P("section", None, None),
        P("section", None),
    )
    return jax.shard_map(
        body,
        mesh=mesh,
        in_specs=placed,
        out_specs=(P("section", None, None, None), P("section", None, None), P("section", None)),
        check_vma=False,
    )
```

```python
import functools

import jax
import jax.numpy as jnp
import numpy as np
from jax import lax
from jax.experimental import pallas as pl
from jax.experimental.pallas import tpu as pltpu
from jax.sharding import PartitionSpec as P

GROUP = 16
LANES = 128
SUB = 128
RING = 4

F32 = jnp.float32
BF16 = jnp.bfloat16


def shifted(array, axis, by):
    count = lax.axis_size(axis)
    pairs = [(i, i + by) for i in range(count) if 0 <= i + by < count]
    return lax.ppermute(array, axis, pairs)


def split(matrix):
    high = matrix.astype(jnp.bfloat16)
    low = (matrix - high.astype(np.float64)).astype(jnp.bfloat16)
    return high, low


@functools.lru_cache(None)
def tables(length, taps):
    points = 2 * length
    pos = np.arange(length)[:, None]
    freq = np.arange(length)[None, :]
    angle = 2.0 * np.pi * ((pos * freq) % points) / points
    real, imag = np.cos(angle), -np.sin(angle)
    imag[:, 0] = 1.0 - 2.0 * (np.arange(length) % 2)
    forward = np.concatenate([real, imag], axis=1)
    weight = np.full((2 * length, 1), 2.0 / points)
    weight[0] = weight[length] = 1.0 / points
    inverse = weight * forward.T
    shift = np.concatenate([np.eye(length, k=lag) for lag in range(1, taps)], axis=1)
    unshift = np.concatenate([np.eye(length, k=-lag) for lag in range(1, taps)], axis=0)
    return (
        np.concatenate(split(forward), axis=0),
        np.concatenate(split(inverse), axis=1),
        shift.astype(jnp.bfloat16),
        unshift.astype(jnp.bfloat16),
    )


def nt(left, right):
    return lax.dot_general(left, right, (((1,), (1,)), ((), ())), preferred_element_type=F32)


def mm(left, right):
    return jnp.dot(left, right, preferred_element_type=F32)


def halves(value):
    high = value.astype(BF16)
    return high, (value - high.astype(F32)).astype(BF16)


def row(ref, *index):
    return jnp.broadcast_to(ref[index], (GROUP, LANES))


def own_channel():
    lane = lax.broadcasted_iota(jnp.int32, (GROUP, LANES), 1)
    return lax.rem(lane, GROUP) == lax.broadcasted_iota(jnp.int32, (GROUP, LANES), 0)


class Tick:
    def __init__(self, last, taps, ins, outs, scratch):
        self.last, self.taps, self.ng = last, taps, SUB // GROUP
        (self.x, self.cot, self.f, self.med, self.skip, self.fwd, self.inv, self.shift) = ins[:8]
        scratch = list(scratch)
        if last:
            self.acc_in, self.skip_in, self.coef, self.columns = ins[8:12]
            self.earlier = ins[12:]
            (self.msg,) = outs
            self.acc, self.skips = scratch.pop(0), scratch.pop(0)
        else:
            (self.unshift,) = ins[8:]
            self.gin, self.acc, self.skips, self.coef, self.columns = outs
            self.turn = scratch.pop(0)
        rings = [scratch[i : i + RING] for i in range(0, len(scratch), RING)]
        (self.taps_at, self.coef_at, self.skip_at, self.xs, self.feat, self.lows, self.hat,
         self.spec, self.res, self.terms, self.sums, self.hats, self.corr, self.base) = rings

    def rows(self, block):
        return pl.multiple_of(block * SUB, SUB)

    def groups(self, block):
        return pl.ds(pl.multiple_of(block * self.ng, self.ng), self.ng)

    def setup(self):
        first = lax.broadcasted_iota(jnp.int32, (1, LANES), 1) == 0
        h = self.med[...].astype(BF16)
        hh = mm(jnp.concatenate([h, h], axis=1), self.fwd[...])
        hr, hi = hh[:, :LANES], hh[:, LANES:]
        self.coef[0] = hr
        self.coef[1] = jnp.where(first, 0.0, hi)
        self.coef[2] = jnp.where(first, hi, hr)
        self.turn[...] = jnp.zeros_like(self.turn)
        for q in range(h.shape[0] // LANES):
            cols = slice(LANES * q, LANES * (q + 1))
            for m in range(3):
                for j in range(self.taps):
                    t = m * self.taps + j
                    self.turn[t : t + 1, :] = self.f[m, j, :, cols]
            self.columns[cols, :] = self.turn[...].T

    def start(self, block, slot):
        taps_at, skip_at, xs = self.taps_at[slot], self.skip_at[slot], self.xs[slot]
        x = self.x[pl.ds(self.rows(block), SUB), :]
        xs[:, LANES:] = mm(x, self.shift[...])
        xs[:, :LANES] = x.astype(F32)
        mine = self.columns[self.groups(block), :]
        for t in range(3 * self.taps):
            taps_at[t] = jnp.broadcast_to(mine[:, t : t + 1], (self.ng, LANES))
        for i in range(3):
            self.coef_at[slot][i] = self.coef[i, self.groups(block), :]
        for q in range(SUB // LANES):
            skip = self.skip[pl.ds(block * (SUB // LANES) + q, 1), :]
            skip_at[LANES * q : LANES * (q + 1)] = jnp.broadcast_to(skip, (LANES, LANES)).T

    def features(self, block, slot):
        taps_at, xs, feat, lows = (r[slot] for r in (self.taps_at, self.xs, self.feat, self.lows))
        for k in range(self.ng):
            r = slice(GROUP * k, GROUP * (k + 1))
            rg = slice(SUB + GROUP * k, SUB + GROUP * (k + 1))
            f = []
            for m in range(3):
                total = None
                for j in range(self.taps):
                    tap = row(taps_at, m * self.taps + j, slice(k, k + 1))
                    term = tap * xs[r, LANES * j : LANES * (j + 1)]
                    total = term if total is None else total + term
                f.append(total)
            product = f[1] * f[2]
            gm = self.cot[pl.ds(self.rows(block) + GROUP * k, GROUP), :].astype(F32) * f[0]
            feat[0, r] = f[1]
            feat[1, r] = f[2]
            feat[2, r] = product
            feat[3, r] = gm
            lows[r] = product.astype(BF16)
            lows[rg] = gm.astype(BF16)
        low = lows[...]
        self.hat[slot][...] = mm(jnp.concatenate([low, low], axis=1), self.fwd[...])

    def filter(self, slot):
        coef_at, hat, spec, terms = (
            r[slot] for r in (self.coef_at, self.hat, self.spec, self.terms)
        )
        for k in range(self.ng):
            r = slice(GROUP * k, GROUP * (k + 1))
            rg = slice(SUB + GROUP * k, SUB + GROUP * (k + 1))
            ca, cb, cc = (row(coef_at, i, slice(k, k + 1)) for i in range(3))
            pr, pi = hat[r, :LANES], hat[r, LANES:]
            gr, gi = hat[rg, :LANES], hat[rg, LANES:]
            spec[r, :LANES] = (pr * ca - pi * cb).astype(BF16)
            spec[r, LANES:] = (pr * cb + pi * cc).astype(BF16)
            spec[rg, :LANES] = (gr * ca + gi * cb).astype(BF16)
            spec[rg, LANES:] = (gi * cc - gr * cb).astype(BF16)
            for i, value in enumerate((pr * gr, pi * gi, pr * gi - pi * gr)):
                terms[i, 8 * k : 8 * k + 8, :] = value[:8] + value[8:]
        wide = mm(spec[...], self.inv[...])
        self.res[slot][...] = wide[:, :LANES] + wide[:, LANES:]

    def gradients(self, block, slot):
        taps_at, skip_at, xs, feat, res, sums, hats, corr = (
            r[slot]
            for r in (self.taps_at, self.skip_at, self.xs, self.feat, self.res, self.sums,
                      self.hats, self.corr)
        )
        for k in range(self.ng):
            r = slice(GROUP * k, GROUP * (k + 1))
            rg = slice(SUB + GROUP * k, SUB + GROUP * (k + 1))
            cot = self.cot[pl.ds(self.rows(block) + GROUP * k, GROUP), :].astype(F32)
            kf, vf, product, gm = (feat[i, r] for i in range(4))
            sk = skip_at[r]
            gq = cot * (res[r] + sk * product)
            gp = res[rg] + sk * gm
            gf = [gq, gp * vf, gp * kf]
            sums[r] = (gm * product).astype(BF16)
            gfb = jnp.concatenate([g.astype(BF16) for g in gf], axis=0)
            xsb = jnp.concatenate(
                [self.x[pl.ds(self.rows(block) + GROUP * k, GROUP), :]]
                + [xs[r, LANES * j : LANES * (j + 1)].astype(BF16) for j in range(1, self.taps)]
                + [jnp.zeros((GROUP, LANES), BF16)] * (LANES // GROUP - self.taps),
                axis=0,
            )
            corr[k] = nt(gfb, xsb)
            if not self.last:
                for j in range(self.taps):
                    total = None
                    for m in range(3):
                        tap = row(taps_at, m * self.taps + j, slice(k, k + 1))
                        total = tap * gf[m] if total is None else total + tap * gf[m]
                    if j == 0:
                        self.base[slot][r] = cot + total
                    else:
                        hats[r, LANES * (j - 1) : LANES * j] = total.astype(BF16)

    def finish(self, block, slot):
        terms, corr = self.terms[slot], self.corr[slot]
        own = own_channel()
        for k in range(self.ng):
            for m in range(3):
                kept = jnp.where(own, corr[k, GROUP * m : GROUP * (m + 1)], 0.0)
                terms[3 + m, 8 * k : 8 * k + 8, :] = kept[:8] + kept[8:]
        for i in range(6):
            total = terms[i, pl.ds(0, self.ng, stride=8), :]
            for s in range(1, 8):
                total = total + terms[i, pl.ds(s, self.ng, stride=8), :]
            self.acc[i, self.groups(block), :] = total
        if not self.last:
            rows = pl.ds(self.rows(block), SUB)
            gin = mm(self.hats[slot][...], self.unshift[...]) + self.base[slot][...]
            self.gin[rows, :] = gin.astype(BF16)
        sums = nt(jnp.ones((8, LANES), BF16), self.sums[slot][...])
        for q in range(SUB // LANES):
            at = pl.ds(block * (SUB // LANES) + q, 1)
            self.skips[at, :] = sums[:1, LANES * q : LANES * (q + 1)]

    def run(self, blocks):
        for t in range(3):
            self.start(t, t % RING)
        for t in range(2):
            self.features(t, t % RING)
        self.filter(0)

        order = "cabde" if self.last else "acdbe"

        def step(t, u, left):
            stages = {
                "a": (3, self.start, t + 3, (u + 3) % RING),
                "b": (2, self.features, t + 2, (u + 2) % RING),
                "c": (1, self.filter, (u + 1) % RING),
                "d": (0, self.gradients, t, u),
                "e": (0, self.finish, jnp.maximum(t - 1, 0), (u - 1) % RING),
            }
            for name in order:
                ahead, stage, *where = stages[name]
                if ahead < left:
                    stage(*where)

        def turn(index, _):
            for u in range(RING):
                step(RING * index + u, u, RING)
            return 0

        lax.fori_loop(0, blocks // RING - 1, turn, 0)
        for u in range(RING):
            step(blocks - RING + u, u, RING - u)
        self.finish(blocks - 1, (blocks - 1) % RING)

    def message(self):
        first = lax.broadcasted_iota(jnp.int32, (1, LANES), 1) == 0
        total = [self.acc[i] + self.acc_in[i] for i in range(6)]
        real = total[0] + jnp.where(first, 0.0, total[1])
        imag = jnp.where(first, total[1], total[2])
        high, low = halves(jnp.concatenate([real, imag], axis=1))
        inv = self.inv[...]
        wide = mm(high, inv)
        medium = wide[:, :LANES] + (wide[:, LANES:] + mm(low, inv[:, :LANES]))
        pick = (
            lax.broadcasted_iota(jnp.int32, (8, LANES), 1) // GROUP
            == lax.broadcasted_iota(jnp.int32, (8, LANES), 0)
        ).astype(BF16)
        pieces = [medium, self.skips[...] + self.skip_in[...]]
        for m in range(3):
            high, low = halves(total[3 + m])
            pieces.append(nt(pick, high) + nt(pick, low))
        pieces.append(jnp.zeros((8, LANES), F32))
        mine = jnp.concatenate(pieces, axis=0).astype(BF16)
        at = 0
        for ref in self.earlier:
            self.msg[: ref.shape[0]] = ref[...]
            at = ref.shape[0]
        self.msg[at : at + mine.shape[0]] = mine


def tick_kernel(last, taps, counts, where, *refs):
    ins, outs, scratch = refs[: counts[0]], refs[counts[0] : sum(counts)], refs[sum(counts) :]
    x, cot, f, med, skip = ins[:5]
    tick, chunk, at, channels = where
    if chunk is None:
        views = (x.at[0, 0, 0], cot, f, med.at[0], skip)
    else:
        groups, rows = channels // GROUP, channels // LANES
        views = (
            x.at[0, tick, 0, pl.ds(chunk * channels, channels), :],
            cot.at[pl.ds(at * channels, channels), :],
            f.at[:, :, :, pl.ds(chunk * groups, groups)],
            med.at[0, pl.ds(chunk * groups, groups), :],
            skip.at[pl.ds(chunk * rows, rows), :],
        )
    work = Tick(last, taps, (*views, *ins[5:]), outs, scratch)
    if not last:
        work.setup()
    work.run(channels // SUB)
    if last:
        work.message()


def in_hbm(array):
    return pltpu.with_memory_space_constraint(array, pltpu.HBM)


def run_tick(saved, cot, filters, medium, skip_rows, tick, chunk, chunks, prior):
    last = prior is not None
    total, length = saved.shape[-2:]
    channels = total // chunks
    taps = filters.shape[1]
    groups = channels // GROUP
    forward, inverse, shift, unshift = tables(length, taps)
    ng = SUB // GROUP
    full = lambda a: pl.BlockSpec(a.shape, lambda i: (0,) * len(a.shape))
    at = chunk if cot.shape[0] == total else 0
    ins = [saved, cot, filters, medium, skip_rows, forward, inverse, shift]
    ins += [] if last else [unshift]
    fetch = not last and chunk == 0
    if fetch:
        ins = [in_hbm(jnp.asarray(a)) for a in ins]
    ins += [*prior] if last else []
    in_specs = [
        pl.BlockSpec((1, 1, 1, channels, length), lambda i: (0, tick, 0, chunk, 0)),
        pl.BlockSpec((channels, length), lambda i: (at, 0)),
        pl.BlockSpec((3, taps, 1, groups), lambda i: (0, 0, 0, chunk)),
        pl.BlockSpec((1, groups, length), lambda i: (0, chunk, 0)),
        pl.BlockSpec((channels // LANES, LANES), lambda i: (chunk, 0)),
    ] + [full(a) for a in ins[5:]]
    whole = pl.BlockSpec(memory_space=pltpu.VMEM)
    if not fetch:
        in_specs = [whole] * len(ins)
    acc_shape = (6, groups, LANES)
    skip_shape = (channels // LANES, LANES)
    ring = [
        pltpu.VMEM((3 * taps, ng, LANES), F32),
        pltpu.VMEM((3, ng, LANES), F32),
        pltpu.VMEM((SUB, LANES), F32),
        pltpu.VMEM((SUB, taps * LANES), F32),
        pltpu.VMEM((4, SUB, LANES), F32),
        pltpu.VMEM((2 * SUB, LANES), BF16),
        pltpu.VMEM((2 * SUB, 2 * LANES), F32),
        pltpu.VMEM((2 * SUB, 2 * LANES), BF16),
        pltpu.VMEM((2 * SUB, LANES), F32),
        pltpu.VMEM((6, 8 * ng, LANES), F32),
        pltpu.VMEM((SUB, LANES), BF16),
        pltpu.VMEM((SUB, (taps - 1) * LANES), BF16),
        pltpu.VMEM((ng, 3 * GROUP, LANES), F32),
        pltpu.VMEM((SUB, LANES), F32),
    ]
    if last:
        scratch = [pltpu.VMEM(acc_shape, F32), pltpu.VMEM(skip_shape, F32)]
    else:
        scratch = [pltpu.VMEM((LANES, LANES), F32)]
    scratch += [ref for ref in ring for _ in range(RING)]
    if last:
        rows = (groups + channels // LANES + 32) * (chunk + 1)
        outs = [jax.ShapeDtypeStruct((rows, LANES), BF16)]
    else:
        outs = [
            jax.ShapeDtypeStruct((channels, length), BF16),
            jax.ShapeDtypeStruct(acc_shape, F32),
            jax.ShapeDtypeStruct(skip_shape, F32),
            jax.ShapeDtypeStruct((3, groups, LANES), F32),
            jax.ShapeDtypeStruct((groups, LANES), F32),
        ]
    return pl.pallas_call(
        functools.partial(
            tick_kernel, last, taps, (len(ins), len(outs)),
            (tick, None if fetch else chunk, at, channels),
        ),
        out_shape=outs,
        grid=(1,),
        in_specs=in_specs,
        out_specs=[whole] * len(outs),
        scratch_shapes=scratch,
        compiler_params=pltpu.CompilerParams(vmem_limit_bytes=48 << 20),
        name="last_tick" if last else "first_tick",
    )(*ins)


def finish_kernel(count, taps, chunks, *refs):
    ins, (short_ref, medium_ref, skip_ref) = refs[:count], refs[count:]
    total = ins[0][...].astype(F32)
    for ref in ins[1:]:
        total = total + ref[...].astype(F32)
    total = total * (1.0 / count)
    groups = medium_ref.shape[0] // chunks
    skips = skip_ref.shape[0] // chunks
    for c in range(chunks):
        at = c * (total.shape[0] // chunks)
        medium_ref[groups * c : groups * (c + 1)] = total[at : at + groups]
        at += groups
        skip_ref[skips * c : skips * (c + 1)] = total[at : at + skips]
        at += skips
        for m in range(3):
            for j in range(taps):
                short_ref[m, j, :, groups * c : groups * (c + 1)] = total[at + j : at + j + 1]
            at += 8


def finish(parts, groups, channels, taps, chunks):
    full = lambda a: pl.BlockSpec(a.shape, lambda i: (0,) * len(a.shape))
    outs = (
        jax.ShapeDtypeStruct((3, taps, 1, groups), F32),
        jax.ShapeDtypeStruct((groups, LANES), F32),
        jax.ShapeDtypeStruct((channels // LANES, LANES), F32),
    )
    return pl.pallas_call(
        functools.partial(finish_kernel, len(parts), taps, chunks),
        out_shape=outs,
        grid=(1,),
        in_specs=[full(a) for a in parts],
        out_specs=tuple(full(a) for a in outs),
        compiler_params=pltpu.CompilerParams(vmem_limit_bytes=8 << 20),
        name="finish",
    )(*parts)


def body(saved, upstream, short_filters, medium_filter, skip):
    channels = saved.shape[-2]
    groups, taps = short_filters.shape[2:]
    replicas = lax.axis_size("replica")
    chunks = groups // LANES
    skip_rows = skip.reshape(channels // LANES, LANES)
    filters = jnp.transpose(short_filters, (1, 3, 0, 2))
    rest = (filters, medium_filter, skip_rows)
    incoming, prior = [], []
    for c in range(chunks):
        gin, *sums = run_tick(saved, upstream[0, 0], *rest, 0, c, chunks, None)
        incoming.append(shifted(gin, "section", -1))
        prior.append(sums)
    message = []
    for c in range(chunks):
        message = run_tick(saved, incoming[c], *rest, 1, c, chunks, (*prior[c], *message))
    even = replicas & (replicas - 1) == 0
    parts = [*message]
    for by in range(1, replicas):
        pairs = [(i, i ^ by if even else (i + by) % replicas) for i in range(replicas)]
        parts.append(lax.ppermute(message[0], "replica", pairs))
    short, medium, skip_grad = finish(parts, groups, channels, taps, chunks)
    return (
        jnp.transpose(short, (2, 0, 3, 1)),
        medium[None],
        skip_grad.reshape(1, channels),
    )


def solution(mesh):
    placed = (
        P("section", None, "replica", None, None),
        P("section", "replica", None, None),
        P("section", None, None, None),
        P("section", None, None),
        P("section", None),
    )
    return jax.shard_map(
        body,
        mesh=mesh,
        in_specs=placed,
        out_specs=(P("section", None, None, None), P("section", None, None), P("section", None)),
        check_vma=False,
    )
```

```python
import functools

import jax
import jax.numpy as jnp
import numpy as np
from jax import lax
from jax.experimental import pallas as pl
from jax.experimental.pallas import tpu as pltpu
from jax.sharding import PartitionSpec as P

GROUP = 16
LANES = 128
SUB = 128
RING = 4

F32 = jnp.float32
BF16 = jnp.bfloat16


def shifted(array, axis, by):
    count = lax.axis_size(axis)
    pairs = [(i, i + by) for i in range(count) if 0 <= i + by < count]
    return lax.ppermute(array, axis, pairs)


def split(matrix):
    high = matrix.astype(jnp.bfloat16)
    low = (matrix - high.astype(np.float64)).astype(jnp.bfloat16)
    return high, low


@functools.lru_cache(None)
def tables(length, taps):
    points = 2 * length
    pos = np.arange(length)[:, None]
    freq = np.arange(length)[None, :]
    angle = 2.0 * np.pi * ((pos * freq) % points) / points
    real, imag = np.cos(angle), -np.sin(angle)
    imag[:, 0] = 1.0 - 2.0 * (np.arange(length) % 2)
    forward = np.concatenate([real, imag], axis=1)
    weight = np.full((2 * length, 1), 2.0 / points)
    weight[0] = weight[length] = 1.0 / points
    inverse = weight * forward.T
    shift = np.concatenate([np.eye(length, k=lag) for lag in range(1, taps)], axis=1)
    unshift = np.concatenate([np.eye(length, k=-lag) for lag in range(1, taps)], axis=0)
    return (
        np.concatenate(split(forward), axis=0),
        np.concatenate(split(inverse), axis=1),
        shift.astype(jnp.bfloat16),
        unshift.astype(jnp.bfloat16),
    )


def nt(left, right):
    return lax.dot_general(left, right, (((1,), (1,)), ((), ())), preferred_element_type=F32)


def mm(left, right):
    return jnp.dot(left, right, preferred_element_type=F32)


def halves(value):
    high = value.astype(BF16)
    return high, (value - high.astype(F32)).astype(BF16)


def row(ref, *index):
    return jnp.broadcast_to(ref[index], (GROUP, LANES))


def own_channel():
    lane = lax.broadcasted_iota(jnp.int32, (GROUP, LANES), 1)
    return lax.rem(lane, GROUP) == lax.broadcasted_iota(jnp.int32, (GROUP, LANES), 0)


class Tick:
    def __init__(self, last, taps, ins, outs, scratch):
        self.last, self.taps, self.ng = last, taps, SUB // GROUP
        (self.x, self.cot, self.f, self.med, self.skip, self.fwd, self.inv, self.shift) = ins[:8]
        scratch = list(scratch)
        if last:
            self.acc_in, self.skip_in, self.coef, self.columns = ins[8:12]
            self.earlier = ins[12:]
            (self.msg,) = outs
            self.acc, self.skips = scratch.pop(0), scratch.pop(0)
        else:
            (self.unshift,) = ins[8:]
            self.gin, self.acc, self.skips, self.coef, self.columns = outs
            self.turn = scratch.pop(0)
        rings = [scratch[i : i + RING] for i in range(0, len(scratch), RING)]
        (self.taps_at, self.coef_at, self.skip_at, self.xs, self.feat, self.lows, self.hat,
         self.spec, self.res, self.terms, self.sums, self.hats, self.corr, self.base) = rings

    def rows(self, block):
        return pl.multiple_of(block * SUB, SUB)

    def groups(self, block):
        return pl.ds(pl.multiple_of(block * self.ng, self.ng), self.ng)

    def setup(self):
        first = lax.broadcasted_iota(jnp.int32, (1, LANES), 1) == 0
        h = self.med[...].astype(BF16)
        hh = mm(jnp.concatenate([h, h], axis=1), self.fwd[...])
        hr, hi = hh[:, :LANES], hh[:, LANES:]
        self.coef[0] = hr
        self.coef[1] = jnp.where(first, 0.0, hi)
        self.coef[2] = jnp.where(first, hi, hr)
        self.turn[...] = jnp.zeros_like(self.turn)
        for q in range(h.shape[0] // LANES):
            cols = slice(LANES * q, LANES * (q + 1))
            for m in range(3):
                for j in range(self.taps):
                    t = m * self.taps + j
                    self.turn[t : t + 1, :] = self.f[m, j, :, cols]
            self.columns[cols, :] = self.turn[...].T

    def start(self, block, slot):
        taps_at, skip_at, xs = self.taps_at[slot], self.skip_at[slot], self.xs[slot]
        x = self.x[pl.ds(self.rows(block), SUB), :]
        xs[:, LANES:] = mm(x, self.shift[...])
        xs[:, :LANES] = x.astype(F32)
        mine = self.columns[self.groups(block), :]
        for t in range(3 * self.taps):
            taps_at[t] = jnp.broadcast_to(mine[:, t : t + 1], (self.ng, LANES))
        for i in range(3):
            self.coef_at[slot][i] = self.coef[i, self.groups(block), :]
        for q in range(SUB // LANES):
            skip = self.skip[pl.ds(block * (SUB // LANES) + q, 1), :]
            skip_at[LANES * q : LANES * (q + 1)] = jnp.broadcast_to(skip, (LANES, LANES)).T

    def features(self, block, slot):
        taps_at, xs, feat, lows = (r[slot] for r in (self.taps_at, self.xs, self.feat, self.lows))
        for k in range(self.ng):
            r = slice(GROUP * k, GROUP * (k + 1))
            rg = slice(SUB + GROUP * k, SUB + GROUP * (k + 1))
            f = []
            for m in range(3):
                total = None
                for j in range(self.taps):
                    tap = row(taps_at, m * self.taps + j, slice(k, k + 1))
                    term = tap * xs[r, LANES * j : LANES * (j + 1)]
                    total = term if total is None else total + term
                f.append(total)
            product = f[1] * f[2]
            gm = self.cot[pl.ds(self.rows(block) + GROUP * k, GROUP), :].astype(F32) * f[0]
            feat[0, r] = f[1]
            feat[1, r] = f[2]
            feat[2, r] = product
            feat[3, r] = gm
            lows[r] = product.astype(BF16)
            lows[rg] = gm.astype(BF16)
        low = lows[...]
        self.hat[slot][...] = mm(jnp.concatenate([low, low], axis=1), self.fwd[...])

    def filter(self, slot):
        coef_at, hat, spec, terms = (
            r[slot] for r in (self.coef_at, self.hat, self.spec, self.terms)
        )
        for k in range(self.ng):
            r = slice(GROUP * k, GROUP * (k + 1))
            rg = slice(SUB + GROUP * k, SUB + GROUP * (k + 1))
            ca, cb, cc = (row(coef_at, i, slice(k, k + 1)) for i in range(3))
            pr, pi = hat[r, :LANES], hat[r, LANES:]
            gr, gi = hat[rg, :LANES], hat[rg, LANES:]
            spec[r, :LANES] = (pr * ca - pi * cb).astype(BF16)
            spec[r, LANES:] = (pr * cb + pi * cc).astype(BF16)
            spec[rg, :LANES] = (gr * ca + gi * cb).astype(BF16)
            spec[rg, LANES:] = (gi * cc - gr * cb).astype(BF16)
            for i, value in enumerate((pr * gr, pi * gi, pr * gi - pi * gr)):
                terms[i, 8 * k : 8 * k + 8, :] = value[:8] + value[8:]
        wide = mm(spec[...], self.inv[...])
        self.res[slot][...] = wide[:, :LANES] + wide[:, LANES:]

    def gradients(self, block, slot):
        taps_at, skip_at, xs, feat, res, sums, hats, corr = (
            r[slot]
            for r in (self.taps_at, self.skip_at, self.xs, self.feat, self.res, self.sums,
                      self.hats, self.corr)
        )
        for k in range(self.ng):
            r = slice(GROUP * k, GROUP * (k + 1))
            rg = slice(SUB + GROUP * k, SUB + GROUP * (k + 1))
            cot = self.cot[pl.ds(self.rows(block) + GROUP * k, GROUP), :].astype(F32)
            kf, vf, product, gm = (feat[i, r] for i in range(4))
            sk = skip_at[r]
            gq = cot * (res[r] + sk * product)
            gp = res[rg] + sk * gm
            gf = [gq, gp * vf, gp * kf]
            sums[r] = (gm * product).astype(BF16)
            gfb = jnp.concatenate([g.astype(BF16) for g in gf], axis=0)
            xsb = jnp.concatenate(
                [self.x[pl.ds(self.rows(block) + GROUP * k, GROUP), :]]
                + [xs[r, LANES * j : LANES * (j + 1)].astype(BF16) for j in range(1, self.taps)]
                + [jnp.zeros((GROUP, LANES), BF16)] * (LANES // GROUP - self.taps),
                axis=0,
            )
            corr[k] = nt(gfb, xsb)
            if not self.last:
                for j in range(self.taps):
                    total = None
                    for m in range(3):
                        tap = row(taps_at, m * self.taps + j, slice(k, k + 1))
                        total = tap * gf[m] if total is None else total + tap * gf[m]
                    if j == 0:
                        self.base[slot][r] = cot + total
                    else:
                        hats[r, LANES * (j - 1) : LANES * j] = total.astype(BF16)

    def finish(self, block, slot):
        terms, corr = self.terms[slot], self.corr[slot]
        own = own_channel()
        for k in range(self.ng):
            for m in range(3):
                kept = jnp.where(own, corr[k, GROUP * m : GROUP * (m + 1)], 0.0)
                terms[3 + m, 8 * k : 8 * k + 8, :] = kept[:8] + kept[8:]
        for i in range(6):
            total = terms[i, pl.ds(0, self.ng, stride=8), :]
            for s in range(1, 8):
                total = total + terms[i, pl.ds(s, self.ng, stride=8), :]
            self.acc[i, self.groups(block), :] = total
        if not self.last:
            rows = pl.ds(self.rows(block), SUB)
            gin = mm(self.hats[slot][...], self.unshift[...]) + self.base[slot][...]
            self.gin[rows, :] = gin.astype(BF16)
        sums = nt(jnp.ones((8, LANES), BF16), self.sums[slot][...])
        for q in range(SUB // LANES):
            at = pl.ds(block * (SUB // LANES) + q, 1)
            self.skips[at, :] = sums[:1, LANES * q : LANES * (q + 1)]

    def run(self, blocks):
        for t in range(3):
            self.start(t, t % RING)
        for t in range(2):
            self.features(t, t % RING)
        self.filter(0)

        order = "cabde" if self.last else "acdbe"

        def step(t, u, left):
            stages = {
                "a": (3, self.start, t + 3, (u + 3) % RING),
                "b": (2, self.features, t + 2, (u + 2) % RING),
                "c": (1, self.filter, (u + 1) % RING),
                "d": (0, self.gradients, t, u),
                "e": (0, self.finish, jnp.maximum(t - 1, 0), (u - 1) % RING),
            }
            for name in order:
                ahead, stage, *where = stages[name]
                if ahead < left:
                    stage(*where)

        def turn(index, _):
            for u in range(RING):
                step(RING * index + u, u, RING)
            return 0

        lax.fori_loop(0, blocks // RING - 1, turn, 0, unroll=self.last)
        for u in range(RING):
            step(blocks - RING + u, u, RING - u)
        self.finish(blocks - 1, (blocks - 1) % RING)

    def message(self):
        first = lax.broadcasted_iota(jnp.int32, (1, LANES), 1) == 0
        total = [self.acc[i] + self.acc_in[i] for i in range(6)]
        real = total[0] + jnp.where(first, 0.0, total[1])
        imag = jnp.where(first, total[1], total[2])
        high, low = halves(jnp.concatenate([real, imag], axis=1))
        inv = self.inv[...]
        wide = mm(high, inv)
        medium = wide[:, :LANES] + (wide[:, LANES:] + mm(low, inv[:, :LANES]))
        pick = (
            lax.broadcasted_iota(jnp.int32, (8, LANES), 1) // GROUP
            == lax.broadcasted_iota(jnp.int32, (8, LANES), 0)
        ).astype(BF16)
        pieces = [medium, self.skips[...] + self.skip_in[...]]
        for m in range(3):
            high, low = halves(total[3 + m])
            pieces.append(nt(pick, high) + nt(pick, low))
        pieces.append(jnp.zeros((8, LANES), F32))
        mine = jnp.concatenate(pieces, axis=0).astype(BF16)
        at = 0
        for ref in self.earlier:
            self.msg[: ref.shape[0]] = ref[...]
            at = ref.shape[0]
        self.msg[at : at + mine.shape[0]] = mine


def tick_kernel(last, taps, counts, where, *refs):
    ins, outs, scratch = refs[: counts[0]], refs[counts[0] : sum(counts)], refs[sum(counts) :]
    x, cot, f, med, skip = ins[:5]
    tick, chunk, at, channels = where
    if chunk is None:
        views = (x.at[0, 0, 0], cot, f, med.at[0], skip)
    else:
        groups, rows = channels // GROUP, channels // LANES
        views = (
            x.at[0, tick, 0, pl.ds(chunk * channels, channels), :],
            cot.at[pl.ds(at * channels, channels), :],
            f.at[:, :, :, pl.ds(chunk * groups, groups)],
            med.at[0, pl.ds(chunk * groups, groups), :],
            skip.at[pl.ds(chunk * rows, rows), :],
        )
    work = Tick(last, taps, (*views, *ins[5:]), outs, scratch)
    if not last:
        work.setup()
    work.run(channels // SUB)
    if last:
        work.message()


def in_hbm(array):
    return pltpu.with_memory_space_constraint(array, pltpu.HBM)


def run_tick(saved, cot, filters, medium, skip_rows, tick, chunk, chunks, prior):
    last = prior is not None
    total, length = saved.shape[-2:]
    channels = total // chunks
    taps = filters.shape[1]
    groups = channels // GROUP
    forward, inverse, shift, unshift = tables(length, taps)
    ng = SUB // GROUP
    full = lambda a: pl.BlockSpec(a.shape, lambda i: (0,) * len(a.shape))
    at = chunk if cot.shape[0] == total else 0
    ins = [saved, cot, filters, medium, skip_rows, forward, inverse, shift]
    ins += [] if last else [unshift]
    fetch = not last and chunk == 0
    if fetch:
        ins = [in_hbm(jnp.asarray(a)) for a in ins]
    ins += [*prior] if last else []
    in_specs = [
        pl.BlockSpec((1, 1, 1, channels, length), lambda i: (0, tick, 0, chunk, 0)),
        pl.BlockSpec((channels, length), lambda i: (at, 0)),
        pl.BlockSpec((3, taps, 1, groups), lambda i: (0, 0, 0, chunk)),
        pl.BlockSpec((1, groups, length), lambda i: (0, chunk, 0)),
        pl.BlockSpec((channels // LANES, LANES), lambda i: (chunk, 0)),
    ] + [full(a) for a in ins[5:]]
    whole = pl.BlockSpec(memory_space=pltpu.VMEM)
    if not fetch:
        in_specs = [whole] * len(ins)
    acc_shape = (6, groups, LANES)
    skip_shape = (channels // LANES, LANES)
    ring = [
        pltpu.VMEM((3 * taps, ng, LANES), F32),
        pltpu.VMEM((3, ng, LANES), F32),
        pltpu.VMEM((SUB, LANES), F32),
        pltpu.VMEM((SUB, taps * LANES), F32),
        pltpu.VMEM((4, SUB, LANES), F32),
        pltpu.VMEM((2 * SUB, LANES), BF16),
        pltpu.VMEM((2 * SUB, 2 * LANES), F32),
        pltpu.VMEM((2 * SUB, 2 * LANES), BF16),
        pltpu.VMEM((2 * SUB, LANES), F32),
        pltpu.VMEM((6, 8 * ng, LANES), F32),
        pltpu.VMEM((SUB, LANES), BF16),
        pltpu.VMEM((SUB, (taps - 1) * LANES), BF16),
        pltpu.VMEM((ng, 3 * GROUP, LANES), F32),
        pltpu.VMEM((SUB, LANES), F32),
    ]
    if last:
        scratch = [pltpu.VMEM(acc_shape, F32), pltpu.VMEM(skip_shape, F32)]
    else:
        scratch = [pltpu.VMEM((LANES, LANES), F32)]
    scratch += [ref for ref in ring for _ in range(RING)]
    if last:
        rows = (groups + channels // LANES + 32) * (chunk + 1)
        outs = [jax.ShapeDtypeStruct((rows, LANES), BF16)]
    else:
        outs = [
            jax.ShapeDtypeStruct((channels, length), BF16),
            jax.ShapeDtypeStruct(acc_shape, F32),
            jax.ShapeDtypeStruct(skip_shape, F32),
            jax.ShapeDtypeStruct((3, groups, LANES), F32),
            jax.ShapeDtypeStruct((groups, LANES), F32),
        ]
    return pl.pallas_call(
        functools.partial(
            tick_kernel, last, taps, (len(ins), len(outs)),
            (tick, None if fetch else chunk, at, channels),
        ),
        out_shape=outs,
        grid=(1,),
        in_specs=in_specs,
        out_specs=[whole] * len(outs),
        scratch_shapes=scratch,
        compiler_params=pltpu.CompilerParams(vmem_limit_bytes=48 << 20),
        name="last_tick" if last else "first_tick",
    )(*ins)


def finish_kernel(count, taps, chunks, *refs):
    ins, (short_ref, medium_ref, skip_ref) = refs[:count], refs[count:]
    total = ins[0][...].astype(F32)
    for ref in ins[1:]:
        total = total + ref[...].astype(F32)
    total = total * (1.0 / count)
    groups = medium_ref.shape[0] // chunks
    skips = skip_ref.shape[0] // chunks
    for c in range(chunks):
        at = c * (total.shape[0] // chunks)
        medium_ref[groups * c : groups * (c + 1)] = total[at : at + groups]
        at += groups
        skip_ref[skips * c : skips * (c + 1)] = total[at : at + skips]
        at += skips
        for m in range(3):
            for j in range(taps):
                short_ref[m, j, :, groups * c : groups * (c + 1)] = total[at + j : at + j + 1]
            at += 8


def finish(parts, groups, channels, taps, chunks):
    full = lambda a: pl.BlockSpec(a.shape, lambda i: (0,) * len(a.shape))
    outs = (
        jax.ShapeDtypeStruct((3, taps, 1, groups), F32),
        jax.ShapeDtypeStruct((groups, LANES), F32),
        jax.ShapeDtypeStruct((channels // LANES, LANES), F32),
    )
    return pl.pallas_call(
        functools.partial(finish_kernel, len(parts), taps, chunks),
        out_shape=outs,
        grid=(1,),
        in_specs=[full(a) for a in parts],
        out_specs=tuple(full(a) for a in outs),
        compiler_params=pltpu.CompilerParams(vmem_limit_bytes=8 << 20),
        name="finish",
    )(*parts)


def body(saved, upstream, short_filters, medium_filter, skip):
    channels = saved.shape[-2]
    groups, taps = short_filters.shape[2:]
    replicas = lax.axis_size("replica")
    chunks = groups // LANES
    skip_rows = skip.reshape(channels // LANES, LANES)
    filters = jnp.transpose(short_filters, (1, 3, 0, 2))
    rest = (filters, medium_filter, skip_rows)
    incoming, prior = [], []
    for c in range(chunks):
        gin, *sums = run_tick(saved, upstream[0, 0], *rest, 0, c, chunks, None)
        incoming.append(shifted(gin, "section", -1))
        prior.append(sums)
    message = []
    for c in range(chunks):
        message = run_tick(saved, incoming[c], *rest, 1, c, chunks, (*prior[c], *message))
    even = replicas & (replicas - 1) == 0
    parts = [*message]
    for by in range(1, replicas):
        pairs = [(i, i ^ by if even else (i + by) % replicas) for i in range(replicas)]
        parts.append(lax.ppermute(message[0], "replica", pairs))
    short, medium, skip_grad = finish(parts, groups, channels, taps, chunks)
    return (
        jnp.transpose(short, (2, 0, 3, 1)),
        medium[None],
        skip_grad.reshape(1, channels),
    )


def solution(mesh):
    placed = (
        P("section", None, "replica", None, None),
        P("section", "replica", None, None),
        P("section", None, None, None),
        P("section", None, None),
        P("section", None),
    )
    return jax.shard_map(
        body,
        mesh=mesh,
        in_specs=placed,
        out_specs=(P("section", None, None, None), P("section", None, None), P("section", None)),
        check_vma=False,
    )
```
